128 devices in a mesh: row: 8 (over z_lo, y), col: 16 (over z_hi, x, core).
Axes of the slice: x: 4, y: 4, z: 4 (z_hi: 2, z_lo: 2; z = z_hi * 2 + z_lo), core: 2. Of those that a mesh axis runs over, the one named last changes fastest.
Arguments:
- observed: float32 [4, 65536], P(None, ('row', 'col')), may hold values from -50 to 50
- tile_values: bfloat16 [256, 32, 256, 256], P('row', 'col'), may hold values from -2.2649514 to 2.2649514
- tile_cols: int32 [256, 32], P('row', 'col'), may hold values from 0 to 255
Outputs:
- solution: float32 [4, 1048576], P(None, ('col', 'row'))
- residual_ratio: float32 [4], replicated
The draws below stay inside these ranges and needn't reach their ends.
All inputs are finite; a program needn't handle non-finite values.
Results may differ from the reference program's by a relative error of at most 0.0021.
Values may be sent and summed in bfloat16 or wider, within the bound.
A program may use at most 128 MiB of HBM per device.

```python
import math
import jax
import jax.numpy as jnp
from jax import lax

TS = 256
KR = 2
NRHS = 4
ITERS = 2
N = 1048576
CB = 256
M = 65536
GROUPS = 32
TILE_ROWS = 256


def rise_factor(count, top_value):
    position = jnp.arange(count, dtype=jnp.float32) / max(count - 1, 1)
    return top_value ** position


def draw_observed(key, part):
    key_base, key_rough = jax.random.split(key)
    tiles_along = M // TS
    roughness = jnp.exp(jax.random.uniform(key_rough, (tiles_along,), jnp.float32, 0.0, math.log(10.0 / 3.0)))
    base_values = jnp.clip(jax.random.normal(key_base, (NRHS, M), jnp.float32), -4.0, 4.0)
    trend = rise_factor(tiles_along, 3.0)
    scales = jnp.repeat(roughness * trend, TS)
    return base_values * scales[None, :]


def draw_tile_values(key, part):
    key_base, key_rough = jax.random.split(key)
    sigma = (GROUPS * TS) ** (-0.5)
    roughness = jnp.exp(jax.random.uniform(key_rough, (TILE_ROWS, GROUPS), jnp.float32, 0.0, math.log(10.0 / 3.0)))
    base_values = jnp.clip(jax.random.normal(key_base, (TILE_ROWS, GROUPS, TS, TS), jnp.float32), -4.0, 4.0)
    top_value = 3.0
    row_scale = rise_factor(TILE_ROWS, top_value)
    col_scale = jnp.repeat(rise_factor(GROUPS // KR, top_value), KR)
    scales = sigma * roughness * row_scale[:, None] * col_scale[None, :]
    return (base_values * scales[:, :, None, None]).astype(jnp.bfloat16)


def place_ends(result, stream_key, least, high):
    longest = result.shape.index(max(result.shape))
    spots = []
    for shift in (0, 1):
        where = [jax.random.randint(jax.random.fold_in(stream_key, axis), (), 0, length) for axis, length in enumerate(result.shape)]
        where[longest] = (where[longest] + shift) % result.shape[longest]
        spots.append(tuple(where))
    return result.at[spots[0]].set(least).at[spots[1]].set(high)


def setup_inputs(seed: int = 0) -> dict:
    keys = jax.random.split(jax.random.key(seed), 4)
    return {
        "observed": draw_observed(jax.random.fold_in(keys[3], 71), 0),
        "tile_values": draw_tile_values(jax.random.fold_in(keys[3], 71), 0),
        "tile_cols": place_ends(jax.random.randint(keys[2], (TILE_ROWS, GROUPS), 0, CB), jax.random.fold_in(keys[2], 1), 0, CB - 1).astype(jnp.int32),
    }


epsilon_sq = 1e-06
group_rows = 8

def column_index(tile_cols):
    offsets = jnp.arange(tile_cols.shape[1], dtype=jnp.int32) // KR * CB
    return (tile_cols + offsets[None, :]).astype(jnp.int32)

def forward_map(tiles_grouped, index_grouped, right_bf):
    panel = right_bf.astype(jnp.float32).reshape(NRHS, N // TS, TS)

    def one_group(inputs):
        block_tiles, block_index = inputs
        picked = panel[:, block_index]
        return jnp.einsum('rktj,nrkj->nrt', block_tiles.astype(jnp.float32), picked)
    pieces = lax.map(one_group, (tiles_grouped, index_grouped))
    return jnp.transpose(pieces, (1, 0, 2, 3)).reshape(NRHS, M)

def adjoint_map(tiles_grouped, index_grouped, left_bf):
    rows_grouped = jnp.transpose(left_bf.astype(jnp.float32).reshape(NRHS, TILE_ROWS // group_rows, group_rows, TS), (1, 0, 2, 3))

    def one_group(running, inputs):
        block_tiles, block_index, block_rows = inputs
        tile_terms = jnp.einsum('rktj,nrt->nrkj', block_tiles.astype(jnp.float32), block_rows)
        return (running.at[:, block_index].add(tile_terms), None)
    initial = jnp.zeros((NRHS, N // TS, TS), jnp.float32)
    running = lax.scan(one_group, initial, (tiles_grouped, index_grouped, rows_grouped))[0]
    return running.reshape(NRHS, N)

def lane_norms(values):
    return jnp.sqrt(lax.optimization_barrier(jnp.sum(values * values, axis=1)) + epsilon_sq)

def reference(observed, tile_values, tile_cols):
    columns = column_index(tile_cols)
    tiles_grouped = tile_values.reshape(TILE_ROWS // group_rows, group_rows, GROUPS, TS, TS)
    index_grouped = columns.reshape(TILE_ROWS // group_rows, group_rows, GROUPS)
    beta_norm = lane_norms(observed)
    first_beta = beta_norm
    left_vec = observed / beta_norm[:, None]
    right_raw = adjoint_map(tiles_grouped, index_grouped, observed.astype(jnp.bfloat16)) / beta_norm[:, None]
    alpha_norm = lane_norms(right_raw)
    right_vec = right_raw / alpha_norm[:, None]
    right_bf = right_raw.astype(jnp.bfloat16)
    phibar = beta_norm
    rhobar = alpha_norm
    direction = right_vec
    solution = jnp.zeros_like(right_vec)
    for iteration in range(ITERS):
        left_raw = forward_map(tiles_grouped, index_grouped, right_bf) / alpha_norm[:, None] - alpha_norm[:, None] * left_vec
        product = adjoint_map(tiles_grouped, index_grouped, left_raw.astype(jnp.bfloat16))
        beta_norm = lane_norms(left_raw)
        right_raw = product / beta_norm[:, None] - beta_norm[:, None] * right_vec
        alpha_norm = lane_norms(right_raw)
        left_vec = left_raw / beta_norm[:, None]
        right_vec = right_raw / alpha_norm[:, None]
        right_bf = right_raw.astype(jnp.bfloat16)
        rho_val = jnp.sqrt(rhobar * rhobar + beta_norm * beta_norm)
        cosine = rhobar / rho_val
        sine_val = beta_norm / rho_val
        theta_val = sine_val * alpha_norm
        rhobar = -cosine * alpha_norm
        phi_val = cosine * phibar
        phibar = sine_val * phibar
        solution = solution + (phi_val / rho_val)[:, None] * direction
        direction = right_vec - (theta_val / rho_val)[:, None] * direction
    return (solution, phibar / first_beta)
```

```python
import functools

import jax
import jax.numpy as jnp
from jax import lax
from jax.experimental import pallas as pl
from jax.experimental.pallas import tpu as pltpu
from jax.sharding import PartitionSpec as P

ITERS = 2
N = 1048576

epsilon_sq = 1e-06

MESH = pl.DeviceIdType.MESH
COL_SUM = jnp.float32
LOAD_PARTS = 8
GROUP = 4
HALVES = 2


def scope(name):
    return jax.named_scope(name)


def norm_of(squares):
    total = jnp.sum(squares, axis=1, keepdims=True)
    return jnp.broadcast_to(jnp.sqrt(total + epsilon_sq), squares.shape)


def sum_of_squares(vectors):
    squares = vectors[0] * vectors[0]
    for vector in vectors[1:]:
        squares = squares + vector * vector
    return squares


def offsets(count):
    if count == 16:
        steps = [(z, x, c) for z in range(2) for x in range(4) for c in range(2)]
        return (8, 2, 1), (2, 4, 2), sorted(steps, key=lambda s: (2 * s[0] + min(s[1], 4 - s[1]), s))
    if count == 8:
        steps = [(z, y, 0) for z in range(2) for y in range(4)]
        return (4, 1, 1), (2, 4, 1), sorted(steps, key=lambda s: (s[0], min(s[1], 4 - s[1]), s))
    return (count, 1, 1), (1, count, 1), [(0, d, 0) for d in range(count)]


def peer_list(me, count):
    strides, sizes, steps = offsets(count)
    places = [lax.rem(lax.div(me, stride), size) for stride, size in zip(strides, sizes)]
    peers = []
    for step in steps:
        peer = 0
        for place, size, stride, d in zip(places, sizes, strides, step):
            if size > 1:
                peer = peer + lax.rem(place + d, size) * stride
        peers.append(peer)
    return peers


def solver_kernel(
    rows, cols, rays, own,
    observed_hbm, columns_hbm, tiles_hbm,
    first_ref, second_ref, left_ref, stats_ref,
    observed_ref, cols_ref, cols_vec, tiles, turned, terms, ray_part, left_panel, voxel_panel, voxel_send, voxel_recv, low_send, low_recv,
    ray_send, ray_recv, norm_col, norm_row, table_vec, table_ref,
    input_sem, load_sem, table_sem, lp_send_sem, lp_recv_sem, vs_send_sem, vs_recv_sem, vp_send_sem, vp_recv_sem,
    lo_send_sem, lo_recv_sem, rs_send_sem, rs_recv_sem, nc_send_sem, nc_recv_sem, nr_send_sem, nr_recv_sem,
):
    f32 = jnp.float32
    bf16 = jnp.bfloat16
    me_row = lax.axis_index("row")
    me_col = lax.axis_index("col")
    row_tiles = tiles.shape[0]
    per_block = tiles.shape[1]
    tile_size = tiles.shape[2]
    half = tile_size // HALVES
    sides = observed_ref.shape[0]
    load_rows = row_tiles // LOAD_PARTS
    flat = row_tiles * per_block
    key_rows = table_vec.shape[0] - per_block
    key_lanes = table_vec.shape[1]
    row_peers = peer_list(me_row, rows)
    col_peers = peer_list(me_col, cols)

    def copy_to(axis, peer, src, dst, send_sem, recv_sem):
        return pltpu.make_async_remote_copy(
            src_ref=src, dst_ref=dst, send_sem=send_sem, recv_sem=recv_sem,
            device_id={axis: peer}, device_id_type=MESH,
        )

    def each(me, count, body):
        def step(d, carry):
            body(lax.rem(me + d, count))
            return carry

        lax.fori_loop(1, count, step, 0)

    def tile_loop(count, unroll, body):
        def step(base, carry):
            for j in range(unroll):
                body(base * unroll + j)
            return carry

        lax.fori_loop(0, count // unroll, step, 0)

    def fold(squares):
        return squares[:, :half] + squares[:, half:]

    def split(value):
        high = value.astype(bf16)
        return high, (value - high.astype(f32)).astype(bf16)

    barrier = pltpu.get_barrier_semaphore()
    each(me_col, cols, lambda p: pl.semaphore_signal(barrier, inc=1, device_id={"col": p}, device_id_type=MESH))
    each(me_row, rows, lambda p: pl.semaphore_signal(barrier, inc=1, device_id={"row": p}, device_id_type=MESH))

    def load_part(part):
        piece = pl.ds(part * load_rows, load_rows)
        return pltpu.make_async_copy(tiles_hbm.at[piece], tiles.at[piece], load_sem.at[part])

    loads = (
        pltpu.make_async_copy(observed_hbm, observed_ref, input_sem.at[0]),
        pltpu.make_async_copy(columns_hbm, cols_ref, input_sem.at[1]),
        pltpu.make_async_copy(columns_hbm, cols_vec, input_sem.at[2]),
    )
    for load in loads:
        load.start()
    for part in range(LOAD_PARTS):
        load_part(part).start()

    def side_tile(i):
        return observed_ref[:, i * tile_size:(i + 1) * tile_size]

    def publish_left(turn, vectors):
        for i, vector in enumerate(vectors):
            left_panel[turn, me_col, i] = vector.astype(bf16)
        high, low = split(fold(sum_of_squares(vectors)))
        left_panel[turn, me_col, rays, :, :half] = high
        left_panel[turn, me_col, rays, :, half:] = low

    def left_copy(turn, peer, slot):
        return copy_to(
            "col", peer, left_panel.at[turn, slot], left_panel.at[turn, slot],
            lp_send_sem.at[turn, peer], lp_recv_sem.at[turn, slot],
        )

    def send_left(turn):
        for p in reversed(col_peers[1:]):
            left_copy(turn, p, me_col).start()

    def make_table():
        columns = cols_vec[...]
        numbers = lax.broadcasted_iota(jnp.int32, columns.shape, 0) * row_tiles + lax.broadcasted_iota(
            jnp.int32, columns.shape, 1
        )
        key_shape = (key_rows, key_lanes)
        keys = lax.broadcasted_iota(jnp.int32, key_shape, 0) * key_lanes + lax.broadcasted_iota(jnp.int32, key_shape, 1)
        before = jnp.zeros_like(columns)
        last = jnp.zeros_like(keys)
        for t in range(flat):
            column = cols_ref[t // row_tiles, t % row_tiles]
            before = jnp.where((columns == column) & (numbers > t), t + 1, before)
            last = jnp.where(keys == column, t + 1, last)
        table_vec[...] = jnp.zeros_like(table_vec)
        table_vec[:key_rows, :] = last
        table_vec[key_rows:, :row_tiles] = before
        copy = pltpu.make_async_copy(table_vec, table_ref, table_sem)
        copy.start()
        copy.wait()

    def last_term(c):
        return table_ref[lax.div(c, key_lanes), lax.rem(c, key_lanes)]

    def turn_part(part):
        load_part(part).wait()
        for j in range(load_rows):
            r = part * load_rows + j
            for h in range(HALVES):
                for k in range(per_block):
                    block = tiles[r, k, :, h * half:(h + 1) * half]
                    turned[r, h, k * half:(k + 1) * half, :] = jnp.transpose(block)

    def adjoint(turn):
        with scope(f"g{turn}"):
            for start in range(0, cols, GROUP):
                group = col_peers[start:start + GROUP]
                for p in group:
                    if p is not col_peers[0]:
                        left_copy(turn, p, p).wait_recv()
                products = []
                for p in group:
                    for i in range(rays):
                        r = p * rays + i
                        row = left_panel[turn, p, i]
                        for k in range(per_block):
                            term = jnp.dot(row, tiles[r, k], preferred_element_type=f32)
                            products.append((1 + k * row_tiles + r, term))
                for t, term in products:
                    for h in range(HALVES):
                        terms[h, t] = term[:, h * half:(h + 1) * half]
        with scope(f"chain{turn}"):
            squares = jnp.zeros((sides, half), f32)
            for p in range(cols):
                squares = squares + left_panel[turn, p, rays, :, :half].astype(f32)
                squares = squares + left_panel[turn, p, rays, :, half:].astype(f32)
            high, low = split(squares)
            for h in range(HALVES):
                terms[h, 0] = jnp.zeros((sides, half), f32)

            def chain(r, k):
                before = table_ref[key_rows + k, r]
                for h in range(HALVES):
                    terms[h, 1 + k * row_tiles + r] = terms[h, 1 + k * row_tiles + r] + terms[h, before]

            for k in range(per_block):
                tile_loop(row_tiles, row_tiles, lambda r: chain(r, k))
        with scope(f"sendsums{turn}"):
            for h in range(HALVES):
                for p in reversed(row_peers[1:]):
                    for i in range(own):
                        voxel_send[turn, h, p, i] = terms[h, last_term(p * own + i)].astype(bf16)
                    if h == 0:
                        voxel_send[turn, h, p, own] = high
                        voxel_send[turn, h, p, own + 1] = low
                    sums_copy(turn, h, p, p, me_row).start()
        voxel_recv[turn, 0, me_row, own] = high
        voxel_recv[turn, 0, me_row, own + 1] = low

    def sums_copy(turn, h, peer, source, slot):
        size = pl.ds(0, own + 2 if h == 0 else own)
        return copy_to(
            "row", peer, voxel_send.at[turn, h, source, size], voxel_recv.at[turn, h, slot, size],
            vs_send_sem.at[turn, h, peer], vs_recv_sem.at[turn, h, slot],
        )

    def voxel_copy(turn, h, peer, slot):
        return copy_to(
            "row", peer, voxel_panel[turn][h].at[slot], voxel_panel[turn][h].at[slot],
            vp_send_sem.at[turn, h, peer], vp_recv_sem.at[turn, h, slot],
        )

    def low_copy(peer, source, slot):
        return copy_to(
            "row", peer, low_send.at[source], low_recv.at[slot], lo_send_sem.at[peer], lo_recv_sem.at[slot]
        )

    def fill_low():
        for p in row_peers[1:]:
            for h in range(HALVES):
                for i in range(own):
                    term = terms[h, last_term(p * own + i)]
                    low_send[p, h, i] = (term - voxel_send[0, h, p, i].astype(f32)).astype(bf16)

    near_rows = row_peers[1:rows // 2]
    far_rows = row_peers[rows // 2:]

    def send_low(peers):
        for p in peers:
            low_copy(p, p, me_row).start()

    def add_low(inverse):
        for p in row_peers[1:]:
            low_copy(p, p, p).wait_recv()

        def one(i):
            for h in range(HALVES):
                total = low_recv[row_peers[1], h, i].astype(f32)
                for p in row_peers[2:]:
                    total = total + low_recv[p, h, i].astype(f32)
                lanes = pl.ds(pl.multiple_of(i * tile_size + h * half, half), half)
                first_ref[:, lanes] = first_ref[:, lanes] + total * inverse

        tile_loop(own, 4, one)

    right_refs = (first_ref, second_ref)

    def finish_right(turn, beta_of, alpha_before):
        beta = None
        for h in range(HALVES):
            with scope(f"waitsums{turn}{h}"):
                for p in row_peers[1:]:
                    sums_copy(turn, h, p, p, p).wait_recv()
            if h == 0:
                beta, inverse, pull = beta_of()
            with scope(f"right{turn}{h}"):
                def one(i, squares, h=h):
                    total = terms[h, last_term(me_row * own + i)]
                    for p in row_peers[1:]:
                        total = total + voxel_recv[turn, h, p, i].astype(f32)
                    lanes = pl.ds(pl.multiple_of(i * tile_size + h * half, half), half)
                    right_raw = total * inverse
                    if turn > 0:
                        right_raw = right_raw - pull * right_refs[turn - 1][:, lanes]
                    right_refs[turn][:, lanes] = right_raw
                    voxel_panel[turn][h][me_row, i] = right_raw.astype(bf16)
                    return squares + right_raw * right_raw

                def step(base, squares):
                    for j in range(4):
                        squares = one(base * 4 + j, squares)
                    return squares

                squares = lax.fori_loop(0, own // 4, step, jnp.zeros((sides, half), f32))
                high, low = split(squares)
                voxel_panel[turn][h][me_row, own] = high
                voxel_panel[turn][h][me_row, own + 1] = low
                for p in reversed(row_peers[1:]):
                    voxel_copy(turn, h, p, me_row).start()
        return beta

    def beta_over_row(turn):
        total = jnp.zeros((sides, half), f32)
        for p in range(rows):
            total = total + voxel_recv[turn, 0, p, own].astype(f32)
            total = total + voxel_recv[turn, 0, p, own + 1].astype(f32)
        return norm_of(total)

    def ray_copy(turn, peer, source, slot):
        return copy_to(
            "col", peer, ray_send.at[turn, source], ray_recv.at[turn, slot],
            rs_send_sem.at[turn, peer], rs_recv_sem.at[turn, slot],
        )

    def picked(turn, h, r):
        pieces = []
        for k in range(per_block):
            c = cols_ref[k, r]
            pieces.append(voxel_panel[turn][h][lax.div(c, own), lax.rem(c, own)])
        return jnp.concatenate(pieces, axis=1)

    def forward(turn):
        with scope(f"waitvox{turn}0"):
            for p in row_peers[1:]:
                voxel_copy(turn, 0, p, p).wait_recv()
        with scope(f"f{turn}0"):
            def early(r):
                ray_part[r] = jnp.dot(picked(turn, 0, r), turned[r, 0], preferred_element_type=f32)

            tile_loop(row_tiles, min(8, row_tiles), early)
        with scope(f"waitvox{turn}1"):
            for p in row_peers[1:]:
                voxel_copy(turn, 1, p, p).wait_recv()
        with scope(f"f{turn}1"):
            squares = jnp.zeros((sides, half), f32)
            for h in range(HALVES):
                for p in range(rows):
                    squares = squares + voxel_panel[turn][h][p, own].astype(f32)
                    squares = squares + voxel_panel[turn][h][p, own + 1].astype(f32)
            farthest = col_peers[::-1]
            for start in range(0, cols, GROUP):
                group = farthest[start:start + GROUP]
                products = []
                for p in group:
                    for i in range(rays):
                        r = p * rays + i
                        total = ray_part[r] + jnp.dot(picked(turn, 1, r), turned[r, 1], preferred_element_type=f32)
                        products.append((p, i, total))
                for p, i, total in products:
                    for h in range(HALVES):
                        ray_send[turn, p, HALVES * i + h] = total[:, h * half:(h + 1) * half]
                for p in group:
                    if p is not col_peers[0]:
                        ray_send[turn, p, HALVES * rays] = squares
                        ray_copy(turn, p, p, me_col).start()
            if turn == 0:
                send_low(near_rows)
            ray_recv[turn, me_col, HALVES * rays] = squares
        with scope(f"waitrays{turn}"):
            pieces = [ray_send[turn, me_col, i] for i in range(HALVES * rays)]
            for p in col_peers[1:]:
                ray_copy(turn, p, p, p).wait_recv()
                for i in range(HALVES * rays):
                    pieces[i] = pieces[i] + ray_recv[turn, p, i]
            squares = ray_recv[turn, 0, HALVES * rays]
            for p in range(1, cols):
                squares = squares + ray_recv[turn, p, HALVES * rays]
        sums = [jnp.concatenate(pieces[HALVES * i:HALVES * (i + 1)], axis=1) for i in range(rays)]
        return sums, norm_of(squares)

    def wide(value):
        return jnp.concatenate([value] * HALVES, axis=1)

    loads[0].wait()
    publish_left(0, [side_tile(i) for i in range(rays)])
    with scope("barrier"):
        pl.semaphore_wait(barrier, rows - 1 + cols - 1)
    send_left(0)
    with scope("table"):
        loads[1].wait()
        loads[2].wait()
        make_table()
    with scope("turn"):
        for part in range(LOAD_PARTS):
            turn_part(part)
    adjoint(0)
    with scope("fill"):
        fill_low()

    def first_beta():
        beta = beta_over_row(0)
        return beta, 1.0 / beta, None

    beta0 = finish_right(0, first_beta, None)
    sums, alpha0 = forward(0)
    alpha = wide(alpha0)
    beta = wide(beta0)
    left_raw = [sums[i] / alpha - alpha * (side_tile(i) / beta) for i in range(rays)]
    for i in range(rays):
        left_ref[i] = left_raw[i]
    publish_left(1, left_raw)
    send_left(1)
    send_low(far_rows)
    adjoint(1)
    with scope("addlow"):
        add_low(1.0 / beta0)

    def second_beta():
        beta = beta_over_row(1)
        return beta, 1.0 / beta, beta / alpha0

    beta1 = finish_right(1, second_beta, alpha0)
    rho1 = jnp.sqrt(alpha0 * alpha0 + beta1 * beta1)
    cosine1 = alpha0 / rho1
    sine1 = beta1 / rho1
    phi1 = cosine1 * beta0
    phibar1 = sine1 * beta0
    sums, alpha1 = forward(1)
    theta1 = sine1 * alpha1
    rhobar1 = -cosine1 * alpha1
    alpha = wide(alpha1)
    beta = wide(beta1)
    left_raw = [sums[i] / alpha - alpha * (left_ref[i] / beta) for i in range(rays)]
    for i in range(rays):
        left_ref[i] = left_raw[i]

    parts = 2 if cols == 16 else 1
    inner = cols // parts
    my_part = lax.div(me_col, inner)
    my_place = lax.rem(me_col, inner)
    place_peers = [(me_row, p, lax.rem(p, inner)) for p in col_peers[1:inner]]
    part_peers = []
    for d in range(parts):
        part = lax.rem(my_part + d, parts)
        for p in row_peers if d else row_peers[1:]:
            part_peers.append((p, part * inner + my_place, part * rows + p))

    def norm_copy(ref, peer, slot, send_sem, recv_sem):
        return pltpu.make_async_remote_copy(
            src_ref=ref.at[slot], dst_ref=ref.at[slot], send_sem=send_sem.at[peer[2]], recv_sem=recv_sem.at[slot],
            device_id={"row": peer[0], "col": peer[1]}, device_id_type=MESH,
        )

    def all_sum(ref, peers, me, value, send_sem, recv_sem):
        ref[me] = value
        for peer in reversed(peers):
            norm_copy(ref, peer, me, send_sem, recv_sem).start()
        for peer in peers:
            norm_copy(ref, peer, peer[2], send_sem, recv_sem).wait_recv()
        total = ref[0]
        for p in range(1, len(peers) + 1):
            total = total + ref[p]
        return total

    squares = fold(sum_of_squares(left_raw))
    with scope("normcol"):
        squares = all_sum(norm_col, place_peers, my_place, squares, nc_send_sem, nc_recv_sem)
    with scope("normrow"):
        squares = all_sum(norm_row, part_peers, my_part * rows + me_row, squares, nr_send_sem, nr_recv_sem)
    beta2 = norm_of(squares)
    rho2 = jnp.sqrt(rhobar1 * rhobar1 + beta2 * beta2)
    cosine2 = rhobar1 / rho2
    sine2 = beta2 / rho2
    phi2 = cosine2 * phibar1
    phibar2 = sine2 * phibar1
    for i, value in enumerate((
        alpha0, alpha1, phi1 / rho1, theta1 / rho1, phi2 / rho2, phibar2 / beta0, beta2, rho2, cosine2, sine2
    )):
        stats_ref[i] = value
    with scope("drain"):
        def drain_row(p):
            for turn in range(ITERS):
                for h in range(HALVES):
                    sums_copy(turn, h, p, p, me_row).wait_send()
                    voxel_copy(turn, h, p, me_row).wait_send()
            low_copy(p, p, me_row).wait_send()

        def drain_col(p):
            for turn in range(ITERS):
                left_copy(turn, p, me_col).wait_send()
                ray_copy(turn, p, p, me_col).wait_send()

        each(me_row, rows, drain_row)
        each(me_col, cols, drain_col)
        for peer in place_peers:
            norm_copy(norm_col, peer, my_place, nc_send_sem, nc_recv_sem).wait_send()
        for peer in part_peers:
            norm_copy(norm_row, peer, my_part * rows + me_row, nr_send_sem, nr_recv_sem).wait_send()


def local(observed, tile_values, tile_cols):
    sides = observed.shape[0]
    row_tiles = tile_values.shape[0]
    per_block = tile_values.shape[1]
    tile_size = tile_values.shape[2]
    rows = lax.axis_size("row")
    cols = lax.axis_size("col")
    col_tiles = N // (tile_size * cols)
    panel_len = col_tiles * tile_size
    own = col_tiles // rows
    rays = row_tiles // cols
    flat = row_tiles * per_block
    half = tile_size // HALVES
    key_lanes = min(col_tiles, 128)
    key_rows = col_tiles // key_lanes

    f32 = jnp.float32
    bf16 = tile_values.dtype
    share_len = own * tile_size
    dma = pltpu.SemaphoreType.DMA
    voxel_shape = (ITERS, HALVES, rows, own + 2, sides, half)
    ray_shape = (ITERS, cols, HALVES * rays + 1, sides, half)
    scratch = [
        pltpu.VMEM(observed.shape, f32),
        pltpu.SMEM(tile_cols.shape[::-1], jnp.int32),
        pltpu.VMEM(tile_cols.shape[::-1], jnp.int32),
        pltpu.VMEM(tile_values.shape, bf16),
        pltpu.VMEM((row_tiles, HALVES, per_block * half, tile_size), bf16),
        pltpu.VMEM((HALVES, 1 + flat, sides, half), f32),
        pltpu.VMEM((row_tiles, sides, tile_size), f32),
        pltpu.VMEM((ITERS, cols, rays + 1, sides, tile_size), bf16),
        [[pltpu.VMEM(voxel_shape[2:], bf16) for _ in range(HALVES)] for _ in range(ITERS)],
        pltpu.VMEM(voxel_shape, bf16),
        pltpu.VMEM(voxel_shape, bf16),
        pltpu.VMEM((rows, HALVES, own, sides, half), bf16),
        pltpu.VMEM((rows, HALVES, own, sides, half), bf16),
        pltpu.VMEM(ray_shape, COL_SUM),
        pltpu.VMEM(ray_shape, COL_SUM),
        pltpu.VMEM((cols, sides, half), f32),
        pltpu.VMEM((2 * rows, sides, half), f32),
        pltpu.VMEM((key_rows + per_block, key_lanes), jnp.int32),
        pltpu.SMEM((key_rows + per_block, key_lanes), jnp.int32),
        dma((3,)), dma((LOAD_PARTS,)), dma,
        dma((ITERS, cols)), dma((ITERS, cols)),
        dma((ITERS, HALVES, rows)), dma((ITERS, HALVES, rows)),
        dma((ITERS, HALVES, rows)), dma((ITERS, HALVES, rows)),
        dma((rows,)), dma((rows,)),
        dma((ITERS, cols)), dma((ITERS, cols)),
        dma((cols,)), dma((cols,)),
        dma((2 * rows,)), dma((2 * rows,)),
    ]
    vmem = pl.BlockSpec(memory_space=pltpu.VMEM)
    hbm = pl.BlockSpec(memory_space=pltpu.HBM)
    columns = jnp.transpose(tile_cols)
    first_raw, second_raw, left_raw, stats = pl.pallas_call(
        functools.partial(solver_kernel, rows, cols, rays, own),
        out_shape=(
            jax.ShapeDtypeStruct((sides, share_len), f32),
            jax.ShapeDtypeStruct((sides, share_len), f32),
            jax.ShapeDtypeStruct((rays, sides, tile_size), f32),
            jax.ShapeDtypeStruct((10, sides, half), f32),
        ),
        in_specs=[hbm, hbm, hbm],
        out_specs=(vmem, vmem, vmem, vmem),
        scratch_shapes=scratch,
        compiler_params=pltpu.CompilerParams(
            collective_id=0, has_side_effects=True, vmem_limit_bytes=57 * 1024 * 1024
        ),
    )(observed, columns, tile_values)

    alpha0, alpha1, step1, turn1, step2, residual_ratio, beta2, rho2, cosine2, sine2 = (
        stats[i, :, :1] for i in range(10)
    )
    direction = first_raw / alpha0
    solution = step1 * direction
    right_vec = second_raw / alpha1
    direction = right_vec - turn1 * direction
    solution = solution + step2 * direction

    left_bf = jnp.transpose(left_raw, (1, 0, 2)).reshape(sides, -1).astype(bf16)
    gathered = lax.all_gather(left_bf, "col", axis=1, tiled=True).reshape(sides, row_tiles, tile_size)
    tile_terms = jnp.einsum("rktj,nrt->nrkj", tile_values, gathered, preferred_element_type=f32)
    placed = (
        jnp.zeros((sides, col_tiles, tile_size), f32)
        .at[:, tile_cols.reshape(-1)]
        .add(tile_terms.reshape(sides, flat, tile_size))
        .reshape(sides, panel_len)
    )
    product = lax.psum_scatter(placed, "row", scatter_dimension=1, tiled=True)
    last_raw = product / beta2 - beta2 * right_vec
    alpha2 = jnp.sqrt(lax.psum(jnp.sum(last_raw * last_raw, axis=1), ("row", "col")) + epsilon_sq)[:, None]
    theta2 = sine2 * alpha2
    rhobar2 = -cosine2 * alpha2
    direction = last_raw / alpha2 - (theta2 / rho2) * direction
    del direction, rhobar2
    return (solution, residual_ratio[:, 0])


def solution(mesh):
    in_specs = (P(None, ("row", "col")), P("row", "col", None, None), P("row", "col"))
    out_specs = (P(None, ("col", "row")), P())
    return jax.shard_map(local, mesh=mesh, in_specs=in_specs, out_specs=out_specs, check_vma=False)
```

```python
import functools

import jax
import jax.numpy as jnp
from jax import lax
from jax.experimental import pallas as pl
from jax.experimental.pallas import tpu as pltpu
from jax.sharding import PartitionSpec as P

ITERS = 2
N = 1048576

epsilon_sq = 1e-06

MESH = pl.DeviceIdType.MESH
COL_SUM = jnp.float32
LOAD_PARTS = 8
GROUP = 4
HALVES = 2


def scope(name):
    return jax.named_scope(name)


def norm_of(squares):
    total = jnp.sum(squares, axis=1, keepdims=True)
    return jnp.broadcast_to(jnp.sqrt(total + epsilon_sq), squares.shape)


def sum_of_squares(vectors):
    squares = vectors[0] * vectors[0]
    for vector in vectors[1:]:
        squares = squares + vector * vector
    return squares


def offsets(count):
    if count == 16:
        steps = [(z, x, c) for z in range(2) for x in range(4) for c in range(2)]
        return (8, 2, 1), (2, 4, 2), sorted(steps, key=lambda s: (2 * s[0] + min(s[1], 4 - s[1]), s))
    if count == 8:
        steps = [(z, y, 0) for z in range(2) for y in range(4)]
        return (4, 1, 1), (2, 4, 1), sorted(steps, key=lambda s: (s[0], min(s[1], 4 - s[1]), s))
    return (count, 1, 1), (1, count, 1), [(0, d, 0) for d in range(count)]


def peer_list(me, count):
    strides, sizes, steps = offsets(count)
    places = [lax.rem(lax.div(me, stride), size) for stride, size in zip(strides, sizes)]
    peers = []
    for step in steps:
        peer = 0
        for place, size, stride, d in zip(places, sizes, strides, step):
            if size > 1:
                peer = peer + lax.rem(place + d, size) * stride
        peers.append(peer)
    return peers


def solver_kernel(
    rows, cols, rays, own,
    observed_ref, cols_vec, tiles_hbm,
    first_ref, second_ref, left_ref, stats_ref,
    cols_ref, tiles, turned, terms, ray_part, left_panel, voxel_panel, voxel_send, voxel_recv, low_send, low_recv,
    ray_send, ray_recv, norm_col, norm_row, table_vec, table_ref,
    columns_sem, load_sem, table_sem, lp_send_sem, lp_recv_sem, vs_send_sem, vs_recv_sem, vp_send_sem, vp_recv_sem,
    lo_send_sem, lo_recv_sem, rs_send_sem, rs_recv_sem, nc_send_sem, nc_recv_sem, nr_send_sem, nr_recv_sem,
):
    f32 = jnp.float32
    bf16 = jnp.bfloat16
    me_row = lax.axis_index("row")
    me_col = lax.axis_index("col")
    row_tiles = tiles.shape[0]
    per_block = tiles.shape[1]
    tile_size = tiles.shape[2]
    half = tile_size // HALVES
    sides = observed_ref.shape[0]
    load_rows = row_tiles // LOAD_PARTS
    flat = row_tiles * per_block
    key_rows = table_vec.shape[0] - per_block
    key_lanes = table_vec.shape[1]
    row_peers = peer_list(me_row, rows)
    col_peers = peer_list(me_col, cols)

    def copy_to(axis, peer, src, dst, send_sem, recv_sem):
        return pltpu.make_async_remote_copy(
            src_ref=src, dst_ref=dst, send_sem=send_sem, recv_sem=recv_sem,
            device_id={axis: peer}, device_id_type=MESH,
        )

    def each(me, count, body):
        def step(d, carry):
            body(lax.rem(me + d, count))
            return carry

        lax.fori_loop(1, count, step, 0)

    def tile_loop(count, unroll, body):
        def step(base, carry):
            for j in range(unroll):
                body(base * unroll + j)
            return carry

        lax.fori_loop(0, count // unroll, step, 0)

    def fold(squares):
        return squares[:, :half] + squares[:, half:]

    def split(value):
        high = value.astype(bf16)
        return high, (value - high.astype(f32)).astype(bf16)

    barrier = pltpu.get_barrier_semaphore()
    each(me_col, cols, lambda p: pl.semaphore_signal(barrier, inc=1, device_id={"col": p}, device_id_type=MESH))
    each(me_row, rows, lambda p: pl.semaphore_signal(barrier, inc=1, device_id={"row": p}, device_id_type=MESH))

    def load_part(part):
        piece = pl.ds(part * load_rows, load_rows)
        return pltpu.make_async_copy(tiles_hbm.at[piece], tiles.at[piece], load_sem.at[part])

    columns_load = pltpu.make_async_copy(cols_vec, cols_ref, columns_sem)
    columns_load.start()
    for part in range(LOAD_PARTS):
        load_part(part).start()

    def side_tile(i):
        return observed_ref[:, i * tile_size:(i + 1) * tile_size]

    def publish_left(turn, vectors):
        for i, vector in enumerate(vectors):
            left_panel[turn, me_col, i] = vector.astype(bf16)
        high, low = split(fold(sum_of_squares(vectors)))
        left_panel[turn, me_col, rays, :, :half] = high
        left_panel[turn, me_col, rays, :, half:] = low

    def left_copy(turn, peer, slot):
        return copy_to(
            "col", peer, left_panel.at[turn, slot], left_panel.at[turn, slot],
            lp_send_sem, lp_recv_sem.at[slot],
        )

    def send_left(turn):
        for p in reversed(col_peers[1:]):
            left_copy(turn, p, me_col).start()

    def make_table():
        columns = cols_vec[...]
        numbers = lax.broadcasted_iota(jnp.int32, columns.shape, 0) * row_tiles + lax.broadcasted_iota(
            jnp.int32, columns.shape, 1
        )
        key_shape = (key_rows, key_lanes)
        keys = lax.broadcasted_iota(jnp.int32, key_shape, 0) * key_lanes + lax.broadcasted_iota(jnp.int32, key_shape, 1)
        before = jnp.zeros_like(columns)
        last = jnp.zeros_like(keys)
        for t in range(flat):
            column = cols_ref[t // row_tiles, t % row_tiles]
            before = jnp.where((columns == column) & (numbers > t), t + 1, before)
            last = jnp.where(keys == column, t + 1, last)
        table_vec[...] = jnp.zeros_like(table_vec)
        table_vec[:key_rows, :] = last
        table_vec[key_rows:, :row_tiles] = before
        copy = pltpu.make_async_copy(table_vec, table_ref, table_sem)
        copy.start()
        copy.wait()

    def last_term(c):
        return table_ref[lax.div(c, key_lanes), lax.rem(c, key_lanes)]

    def turn_part(part):
        load_part(part).wait()
        for j in range(load_rows):
            r = part * load_rows + j
            for h in range(HALVES):
                for k in range(per_block):
                    block = tiles[r, k, :, h * half:(h + 1) * half]
                    turned[r, h, k * half:(k + 1) * half, :] = jnp.transpose(block)

    def adjoint(turn):
        with scope(f"g{turn}"):
            for start in range(0, cols, GROUP):
                group = col_peers[start:start + GROUP]
                for p in group:
                    if p is not col_peers[0]:
                        left_copy(turn, p, p).wait_recv()
                products = []
                for p in group:
                    for i in range(rays):
                        r = p * rays + i
                        row = left_panel[turn, p, i]
                        for k in range(per_block):
                            term = jnp.dot(row, tiles[r, k], preferred_element_type=f32)
                            products.append((1 + k * row_tiles + r, term))
                for t, term in products:
                    for h in range(HALVES):
                        terms[h, t] = term[:, h * half:(h + 1) * half]
        with scope(f"chain{turn}"):
            squares = jnp.zeros((sides, half), f32)
            for p in range(cols):
                squares = squares + left_panel[turn, p, rays, :, :half].astype(f32)
                squares = squares + left_panel[turn, p, rays, :, half:].astype(f32)
            high, low = split(squares)
            for h in range(HALVES):
                terms[h, 0] = jnp.zeros((sides, half), f32)

            def chain(r, k):
                before = table_ref[key_rows + k, r]
                for h in range(HALVES):
                    terms[h, 1 + k * row_tiles + r] = terms[h, 1 + k * row_tiles + r] + terms[h, before]

            for k in range(per_block):
                tile_loop(row_tiles, row_tiles, lambda r: chain(r, k))
        with scope(f"sendsums{turn}"):
            for h in range(HALVES):
                for p in reversed(row_peers[1:]):
                    for i in range(own):
                        voxel_send[turn, h, p, i] = terms[h, last_term(p * own + i)].astype(bf16)
                    if h == 0:
                        voxel_send[turn, h, p, own] = high
                        voxel_send[turn, h, p, own + 1] = low
                    sums_copy(turn, h, p, p, me_row).start()
        voxel_recv[turn, 0, me_row, own] = high
        voxel_recv[turn, 0, me_row, own + 1] = low

    def sums_copy(turn, h, peer, source, slot):
        size = pl.ds(0, own + 2 if h == 0 else own)
        return copy_to(
            "row", peer, voxel_send.at[turn, h, source, size], voxel_recv.at[turn, h, slot, size],
            vs_send_sem.at[h], vs_recv_sem.at[h],
        )

    def voxel_copy(turn, h, peer, slot):
        return copy_to(
            "row", peer, voxel_panel[turn][h].at[slot], voxel_panel[turn][h].at[slot],
            vp_send_sem.at[h], vp_recv_sem.at[h],
        )

    def all_left(turn):
        whole = left_panel.at[turn, pl.ds(0, cols - 1)]
        return copy_to("col", col_peers[1], whole, whole, lp_send_sem, lp_recv_sem.at[0])

    def all_sums(turn, h):
        size = pl.ds(0, own + 2 if h == 0 else own)
        return copy_to(
            "row", row_peers[1], voxel_send.at[turn, h, pl.ds(0, rows - 1), size],
            voxel_recv.at[turn, h, pl.ds(0, rows - 1), size], vs_send_sem.at[h], vs_recv_sem.at[h],
        )

    def all_voxels(turn, h):
        whole = voxel_panel[turn][h].at[pl.ds(0, rows - 1)]
        return copy_to("row", row_peers[1], whole, whole, vp_send_sem.at[h], vp_recv_sem.at[h])

    def all_rays(turn):
        return copy_to(
            "col", col_peers[1], ray_send.at[turn, pl.ds(0, cols - 1)], ray_recv.at[turn, pl.ds(0, cols - 1)],
            rs_send_sem, rs_recv_sem,
        )

    def all_low(group):
        size = pl.ds(0, len(low_groups[group]))
        return copy_to(
            "row", row_peers[1], low_send.at[size], low_recv.at[size], lo_send_sem.at[group], lo_recv_sem.at[group]
        )

    def low_copy(group, peer, source, slot):
        return copy_to(
            "row", peer, low_send.at[source], low_recv.at[slot], lo_send_sem.at[group], lo_recv_sem.at[group]
        )

    def fill_low():
        for p in row_peers[1:]:
            for h in range(HALVES):
                for i in range(own):
                    term = terms[h, last_term(p * own + i)]
                    low_send[p, h, i] = (term - voxel_send[0, h, p, i].astype(f32)).astype(bf16)

    low_groups = (row_peers[1:max(rows // 2, 1)], row_peers[max(rows // 2, 1):])

    def send_low(group):
        for p in low_groups[group]:
            low_copy(group, p, p, me_row).start()

    def low_sum(group, h, i):
        total = low_recv[low_groups[group][0], h, i].astype(f32)
        for p in low_groups[group][1:]:
            total = total + low_recv[p, h, i].astype(f32)
        return total

    def add_low(group, inverse, pull=None):
        if not low_groups[group]:
            return
        all_low(group).wait_recv()

        def one(i):
            for h in range(HALVES):
                lanes = pl.ds(pl.multiple_of(i * tile_size + h * half, half), half)
                change = low_sum(group, h, i) * inverse
                first_ref[:, lanes] = first_ref[:, lanes] + change
                if pull is not None:
                    second_ref[:, lanes] = second_ref[:, lanes] - pull * change

        tile_loop(own, 4, one)

    right_refs = (first_ref, second_ref)

    def finish_right(turn, beta_of, alpha_before):
        beta = None
        for h in range(HALVES):
            with scope(f"waitsums{turn}{h}"):
                all_sums(turn, h).wait_recv()
            if h == 0:
                beta, inverse, pull = beta_of()
            with scope(f"right{turn}{h}"):
                def one(i, squares, h=h):
                    total = terms[h, last_term(me_row * own + i)]
                    for p in row_peers[1:]:
                        total = total + voxel_recv[turn, h, p, i].astype(f32)
                    lanes = pl.ds(pl.multiple_of(i * tile_size + h * half, half), half)
                    right_raw = total * inverse
                    if turn > 0:
                        right_raw = right_raw - pull * right_refs[turn - 1][:, lanes]
                    right_refs[turn][:, lanes] = right_raw
                    voxel_panel[turn][h][me_row, i] = right_raw.astype(bf16)
                    return squares + right_raw * right_raw

                def step(base, squares):
                    for j in range(4):
                        squares = one(base * 4 + j, squares)
                    return squares

                squares = lax.fori_loop(0, own // 4, step, jnp.zeros((sides, half), f32))
                high, low = split(squares)
                voxel_panel[turn][h][me_row, own] = high
                voxel_panel[turn][h][me_row, own + 1] = low
                for p in reversed(row_peers[1:]):
                    voxel_copy(turn, h, p, me_row).start()
        return beta

    def beta_over_row(turn):
        total = jnp.zeros((sides, half), f32)
        for p in range(rows):
            total = total + voxel_recv[turn, 0, p, own].astype(f32)
            total = total + voxel_recv[turn, 0, p, own + 1].astype(f32)
        return norm_of(total)

    def ray_copy(turn, peer, source, slot):
        return copy_to(
            "col", peer, ray_send.at[turn, source], ray_recv.at[turn, slot],
            rs_send_sem, rs_recv_sem,
        )

    def picked(turn, h, r):
        pieces = []
        for k in range(per_block):
            c = cols_ref[k, r]
            pieces.append(voxel_panel[turn][h][lax.div(c, own), lax.rem(c, own)])
        return jnp.concatenate(pieces, axis=1)

    def forward(turn):
        with scope(f"waitvox{turn}0"):
            all_voxels(turn, 0).wait_recv()
        with scope(f"f{turn}0"):
            def early(r):
                ray_part[r] = jnp.dot(picked(turn, 0, r), turned[r, 0], preferred_element_type=f32)

            tile_loop(row_tiles, min(8, row_tiles), early)
        with scope(f"waitvox{turn}1"):
            all_voxels(turn, 1).wait_recv()
        with scope(f"f{turn}1"):
            squares = jnp.zeros((sides, half), f32)
            for h in range(HALVES):
                for p in range(rows):
                    squares = squares + voxel_panel[turn][h][p, own].astype(f32)
                    squares = squares + voxel_panel[turn][h][p, own + 1].astype(f32)
            farthest = col_peers[::-1]
            for start in range(0, cols, GROUP):
                group = farthest[start:start + GROUP]
                products = []
                for p in group:
                    for i in range(rays):
                        r = p * rays + i
                        total = ray_part[r] + jnp.dot(picked(turn, 1, r), turned[r, 1], preferred_element_type=f32)
                        products.append((p, i, total))
                for p, i, total in products:
                    for h in range(HALVES):
                        ray_send[turn, p, HALVES * i + h] = total[:, h * half:(h + 1) * half]
                for p in group:
                    if p is not col_peers[0]:
                        ray_send[turn, p, HALVES * rays] = squares
                        ray_copy(turn, p, p, me_col).start()
            if turn == 0:
                send_low(0)
            ray_recv[turn, me_col, HALVES * rays] = squares
        with scope(f"waitrays{turn}"):
            pieces = [ray_send[turn, me_col, i] for i in range(HALVES * rays)]
            all_rays(turn).wait_recv()
            for p in col_peers[1:]:
                for i in range(HALVES * rays):
                    pieces[i] = pieces[i] + ray_recv[turn, p, i]
            squares = ray_recv[turn, 0, HALVES * rays]
            for p in range(1, cols):
                squares = squares + ray_recv[turn, p, HALVES * rays]
        sums = [jnp.concatenate(pieces[HALVES * i:HALVES * (i + 1)], axis=1) for i in range(rays)]
        return sums, norm_of(squares)

    def wide(value):
        return jnp.concatenate([value] * HALVES, axis=1)

    def drain(turn):
        all_left(turn).wait_send()
        for h in range(HALVES):
            all_sums(turn, h).wait_send()
            all_voxels(turn, h).wait_send()
        all_rays(turn).wait_send()

    publish_left(0, [side_tile(i) for i in range(rays)])
    with scope("barrier"):
        pl.semaphore_wait(barrier, rows - 1 + cols - 1)
    send_left(0)
    with scope("table"):
        columns_load.wait()
        make_table()
    with scope("turn"):
        for part in range(LOAD_PARTS):
            turn_part(part)
    adjoint(0)
    with scope("fill"):
        fill_low()

    def first_beta():
        beta = beta_over_row(0)
        return beta, 1.0 / beta, None

    beta0 = finish_right(0, first_beta, None)
    sums, alpha0 = forward(0)
    alpha = wide(alpha0)
    beta = wide(beta0)
    left_raw = [sums[i] / alpha - alpha * (side_tile(i) / beta) for i in range(rays)]
    for i in range(rays):
        left_ref[i] = left_raw[i]
    publish_left(1, left_raw)
    drain(0)
    send_left(1)
    adjoint(1)
    with scope("addlow"):
        add_low(0, 1.0 / beta0)

    def second_beta():
        beta = beta_over_row(1)
        return beta, 1.0 / beta, beta / alpha0

    beta1 = finish_right(1, second_beta, alpha0)
    rho1 = jnp.sqrt(alpha0 * alpha0 + beta1 * beta1)
    cosine1 = alpha0 / rho1
    sine1 = beta1 / rho1
    phi1 = cosine1 * beta0
    phibar1 = sine1 * beta0
    sums, alpha1 = forward(1)
    theta1 = sine1 * alpha1
    rhobar1 = -cosine1 * alpha1
    alpha = wide(alpha1)
    beta = wide(beta1)
    left_raw = [sums[i] / alpha - alpha * (left_ref[i] / beta) for i in range(rays)]
    for i in range(rays):
        left_ref[i] = left_raw[i]

    parts = 2 if cols == 16 else 1
    inner = cols // parts
    my_part = lax.div(me_col, inner)
    my_place = lax.rem(me_col, inner)
    place_peers = [(me_row, p, lax.rem(p, inner)) for p in col_peers[1:inner]]
    part_peers = []
    for d in range(parts):
        part = lax.rem(my_part + d, parts)
        for p in row_peers if d else row_peers[1:]:
            part_peers.append((p, part * inner + my_place, part * rows + p))

    def norm_copy(ref, peer, slot, send_sem, recv_sem):
        return pltpu.make_async_remote_copy(
            src_ref=ref.at[slot], dst_ref=ref.at[slot], send_sem=send_sem, recv_sem=recv_sem,
            device_id={"row": peer[0], "col": peer[1]}, device_id_type=MESH,
        )

    def all_sum(ref, peers, me, value, send_sem, recv_sem):
        ref[me] = value
        for peer in reversed(peers):
            norm_copy(ref, peer, me, send_sem, recv_sem).start()
        norm_copy(ref, peers[0], pl.ds(0, len(peers)), send_sem, recv_sem).wait()
        total = ref[0]
        for p in range(1, len(peers) + 1):
            total = total + ref[p]
        return total

    squares = fold(sum_of_squares(left_raw))
    send_low(1)
    with scope("normcol"):
        squares = all_sum(norm_col, place_peers, my_place, squares, nc_send_sem, nc_recv_sem)
    with scope("normrow"):
        squares = all_sum(norm_row, part_peers, my_part * rows + me_row, squares, nr_send_sem, nr_recv_sem)
    with scope("addlow2"):
        add_low(1, 1.0 / beta0, beta1 / alpha0)
    beta2 = norm_of(squares)
    rho2 = jnp.sqrt(rhobar1 * rhobar1 + beta2 * beta2)
    cosine2 = rhobar1 / rho2
    sine2 = beta2 / rho2
    phi2 = cosine2 * phibar1
    phibar2 = sine2 * phibar1
    for i, value in enumerate((
        alpha0, alpha1, phi1 / rho1, theta1 / rho1, phi2 / rho2, phibar2 / beta0, beta2, rho2, cosine2, sine2
    )):
        stats_ref[i] = value
    with scope("drain"):
        drain(1)
        for group in range(2):
            if low_groups[group]:
                all_low(group).wait_send()


def local(observed, tile_values, tile_cols):
    sides = observed.shape[0]
    row_tiles = tile_values.shape[0]
    per_block = tile_values.shape[1]
    tile_size = tile_values.shape[2]
    rows = lax.axis_size("row")
    cols = lax.axis_size("col")
    col_tiles = N // (tile_size * cols)
    panel_len = col_tiles * tile_size
    own = col_tiles // rows
    rays = row_tiles // cols
    flat = row_tiles * per_block
    half = tile_size // HALVES
    key_lanes = min(col_tiles, 128)
    key_rows = col_tiles // key_lanes

    f32 = jnp.float32
    bf16 = tile_values.dtype
    share_len = own * tile_size
    dma = pltpu.SemaphoreType.DMA
    voxel_shape = (ITERS, HALVES, rows, own + 2, sides, half)
    ray_shape = (ITERS, cols, HALVES * rays + 1, sides, half)
    scratch = [
        pltpu.SMEM(tile_cols.shape[::-1], jnp.int32),
        pltpu.VMEM(tile_values.shape, bf16),
        pltpu.VMEM((row_tiles, HALVES, per_block * half, tile_size), bf16),
        pltpu.VMEM((HALVES, 1 + flat, sides, half), f32),
        pltpu.VMEM((row_tiles, sides, tile_size), f32),
        pltpu.VMEM((ITERS, cols, rays + 1, sides, tile_size), bf16),
        [[pltpu.VMEM(voxel_shape[2:], bf16) for _ in range(HALVES)] for _ in range(ITERS)],
        pltpu.VMEM(voxel_shape, bf16),
        pltpu.VMEM(voxel_shape, bf16),
        pltpu.VMEM((rows, HALVES, own, sides, half), bf16),
        pltpu.VMEM((rows, HALVES, own, sides, half), bf16),
        pltpu.VMEM(ray_shape, COL_SUM),
        pltpu.VMEM(ray_shape, COL_SUM),
        pltpu.VMEM((cols, sides, half), f32),
        pltpu.VMEM((2 * rows, sides, half), f32),
        pltpu.VMEM((key_rows + per_block, key_lanes), jnp.int32),
        pltpu.SMEM((key_rows + per_block, key_lanes), jnp.int32),
        dma, dma((LOAD_PARTS,)), dma,
        dma, dma((cols,)),
        dma((HALVES,)), dma((HALVES,)),
        dma((HALVES,)), dma((HALVES,)),
        dma((2,)), dma((2,)),
        dma, dma,
        dma, dma,
        dma, dma,
    ]
    vmem = pl.BlockSpec(memory_space=pltpu.VMEM)
    columns = jnp.transpose(tile_cols)
    first_raw, second_raw, left_raw, stats = pl.pallas_call(
        functools.partial(solver_kernel, rows, cols, rays, own),
        out_shape=(
            jax.ShapeDtypeStruct((sides, share_len), f32),
            jax.ShapeDtypeStruct((sides, share_len), f32),
            jax.ShapeDtypeStruct((rays, sides, tile_size), f32),
            jax.ShapeDtypeStruct((10, sides, half), f32),
        ),
        in_specs=[vmem, vmem, pl.BlockSpec(memory_space=pltpu.HBM)],
        out_specs=(vmem, vmem, vmem, vmem),
        scratch_shapes=scratch,
        compiler_params=pltpu.CompilerParams(
            collective_id=0, has_side_effects=True, vmem_limit_bytes=53 * 1024 * 1024
        ),
    )(observed, columns, tile_values)

    alpha0, alpha1, step1, turn1, step2, residual_ratio, beta2, rho2, cosine2, sine2 = (
        stats[i, :, :1] for i in range(10)
    )
    direction = first_raw / alpha0
    solution = step1 * direction
    right_vec = second_raw / alpha1
    direction = right_vec - turn1 * direction
    solution = solution + step2 * direction

    left_bf = jnp.transpose(left_raw, (1, 0, 2)).reshape(sides, -1).astype(bf16)
    gathered = lax.all_gather(left_bf, "col", axis=1, tiled=True).reshape(sides, row_tiles, tile_size)
    tile_terms = jnp.einsum("rktj,nrt->nrkj", tile_values, gathered, preferred_element_type=f32)
    placed = (
        jnp.zeros((sides, col_tiles, tile_size), f32)
        .at[:, tile_cols.reshape(-1)]
        .add(tile_terms.reshape(sides, flat, tile_size))
        .reshape(sides, panel_len)
    )
    product = lax.psum_scatter(placed, "row", scatter_dimension=1, tiled=True)
    last_raw = product / beta2 - beta2 * right_vec
    alpha2 = jnp.sqrt(lax.psum(jnp.sum(last_raw * last_raw, axis=1), ("row", "col")) + epsilon_sq)[:, None]
    theta2 = sine2 * alpha2
    rhobar2 = -cosine2 * alpha2
    direction = last_raw / alpha2 - (theta2 / rho2) * direction
    del direction, rhobar2
    return (solution, residual_ratio[:, 0])


def solution(mesh):
    in_specs = (P(None, ("row", "col")), P("row", "col", None, None), P("row", "col"))
    out_specs = (P(None, ("col", "row")), P())
    return jax.shard_map(local, mesh=mesh, in_specs=in_specs, out_specs=out_specs, check_vma=False)
```

```python
import functools

import jax
import jax.numpy as jnp
from jax import lax
from jax.experimental import pallas as pl
from jax.experimental.pallas import tpu as pltpu
from jax.sharding import PartitionSpec as P

ITERS = 2
N = 1048576

epsilon_sq = 1e-06

MESH = pl.DeviceIdType.MESH
COL_SUMS = (jnp.float32, jnp.bfloat16)
LOAD_PARTS = 8
GROUP = 4
HALVES = 2
STEPS = 2


def scope(name):
    return jax.named_scope(name)


def norm_of(squares):
    total = jnp.sum(squares, axis=1, keepdims=True)
    return jnp.broadcast_to(jnp.sqrt(total + epsilon_sq), squares.shape)


def sum_of_squares(vectors):
    squares = vectors[0] * vectors[0]
    for vector in vectors[1:]:
        squares = squares + vector * vector
    return squares


def offsets(count):
    if count == 16:
        steps = [(z, x, c) for z in range(2) for x in range(4) for c in range(2)]
        return (8, 2, 1), (2, 4, 2), sorted(steps, key=lambda s: (2 * s[0] + min(s[1], 4 - s[1]), s))
    if count == 8:
        steps = [(z, y, 0) for z in range(2) for y in range(4)]
        return (4, 1, 1), (2, 4, 1), sorted(steps, key=lambda s: (s[0], min(s[1], 4 - s[1]), s))
    return (count, 1, 1), (1, count, 1), [(0, d, 0) for d in range(count)]


def peer_list(me, count):
    strides, sizes, steps = offsets(count)
    places = [lax.rem(lax.div(me, stride), size) for stride, size in zip(strides, sizes)]
    peers = []
    for step in steps:
        peer = 0
        for place, size, stride, d in zip(places, sizes, strides, step):
            if size > 1:
                peer = peer + lax.rem(place + d, size) * stride
        peers.append(peer)
    return peers


def solver_kernel(
    rows, cols, rays, own,
    observed_ref, cols_vec, tiles_hbm,
    first_ref, second_ref, left_ref, stats_ref,
    cols_ref, tiles, turned, terms, ray_part, left_panel, voxel_panel, voxel_send, voxel_recv, low_send, low_recv,
    ray_send, ray_recv, norm_col, norm_row, table_vec, table_ref,
    columns_sem, load_sem, table_sem, lp_send_sem, lp_recv_sem, vs_send_sem, vs_recv_sem, vp_send_sem, vp_recv_sem,
    lo_send_sem, lo_recv_sem, rs_send_sem, rs_recv_sem, nc_send_sem, nc_recv_sem, nr_send_sem, nr_recv_sem,
):
    f32 = jnp.float32
    bf16 = jnp.bfloat16
    me_row = lax.axis_index("row")
    me_col = lax.axis_index("col")
    row_tiles = tiles.shape[0]
    per_block = tiles.shape[1]
    tile_size = tiles.shape[2]
    half = tile_size // HALVES
    sides = observed_ref.shape[0]
    load_rows = row_tiles // LOAD_PARTS
    step_tiles = own // STEPS
    chunks = [(h, g) for h in range(HALVES) for g in range(STEPS)]
    flat = row_tiles * per_block
    key_rows = table_vec.shape[0] - per_block
    key_lanes = table_vec.shape[1]
    row_peers = peer_list(me_row, rows)
    col_peers = peer_list(me_col, cols)

    def copy_to(axis, peer, src, dst, send_sem, recv_sem):
        return pltpu.make_async_remote_copy(
            src_ref=src, dst_ref=dst, send_sem=send_sem, recv_sem=recv_sem,
            device_id={axis: peer}, device_id_type=MESH,
        )

    def each(me, count, body):
        def step(d, carry):
            body(lax.rem(me + d, count))
            return carry

        lax.fori_loop(1, count, step, 0)

    def tile_loop(count, unroll, body):
        def step(base, carry):
            for j in range(unroll):
                body(base * unroll + j)
            return carry

        lax.fori_loop(0, count // unroll, step, 0)

    def fold(squares):
        return squares[:, :half] + squares[:, half:]

    def split(value):
        high = value.astype(bf16)
        return high, (value - high.astype(f32)).astype(bf16)

    barrier = pltpu.get_barrier_semaphore()
    each(me_col, cols, lambda p: pl.semaphore_signal(barrier, inc=1, device_id={"col": p}, device_id_type=MESH))
    each(me_row, rows, lambda p: pl.semaphore_signal(barrier, inc=1, device_id={"row": p}, device_id_type=MESH))

    def load_part(part):
        piece = pl.ds(part * load_rows, load_rows)
        return pltpu.make_async_copy(tiles_hbm.at[piece], tiles.at[piece], load_sem.at[part])

    columns_load = pltpu.make_async_copy(cols_vec, cols_ref, columns_sem)
    columns_load.start()
    for part in range(LOAD_PARTS):
        load_part(part).start()

    def side_tile(i):
        return observed_ref[:, i * tile_size:(i + 1) * tile_size]

    def publish_left(turn, vectors):
        for i, vector in enumerate(vectors):
            left_panel[turn, me_col, i] = vector.astype(bf16)
        high, low = split(fold(sum_of_squares(vectors)))
        left_panel[turn, me_col, rays, :, :half] = high
        left_panel[turn, me_col, rays, :, half:] = low

    def left_copy(turn, peer, slot):
        return copy_to(
            "col", peer, left_panel.at[turn, slot], left_panel.at[turn, slot],
            lp_send_sem, lp_recv_sem.at[slot],
        )

    def send_left(turn):
        for p in reversed(col_peers[1:]):
            left_copy(turn, p, me_col).start()

    def make_table():
        columns = cols_vec[...]
        numbers = lax.broadcasted_iota(jnp.int32, columns.shape, 0) * row_tiles + lax.broadcasted_iota(
            jnp.int32, columns.shape, 1
        )
        key_shape = (key_rows, key_lanes)
        keys = lax.broadcasted_iota(jnp.int32, key_shape, 0) * key_lanes + lax.broadcasted_iota(jnp.int32, key_shape, 1)
        before = jnp.zeros_like(columns)
        last = jnp.zeros_like(keys)
        for t in range(flat):
            column = cols_ref[t // row_tiles, t % row_tiles]
            before = jnp.where((columns == column) & (numbers > t), t + 1, before)
            last = jnp.where(keys == column, t + 1, last)
        table_vec[...] = jnp.zeros_like(table_vec)
        table_vec[:key_rows, :] = last
        table_vec[key_rows:, :row_tiles] = before
        copy = pltpu.make_async_copy(table_vec, table_ref, table_sem)
        copy.start()
        copy.wait()

    def share_of(p):
        return lax.div(p * own, key_lanes), lax.rem(p * own, key_lanes)

    def last_term(share, i):
        return table_ref[share[0], share[1] + i]

    def place_of(c):
        if own & (own - 1):
            return lax.div(c, own), lax.rem(c, own)
        return lax.shift_right_logical(c, own.bit_length() - 1), c & (own - 1)

    def turn_part(part):
        for j in range(load_rows):
            r = part * load_rows + j
            for h in range(HALVES):
                for k in range(per_block):
                    block = tiles[r, k, :, h * half:(h + 1) * half]
                    turned[r, h, k * half:(k + 1) * half, :] = jnp.transpose(block)

    def adjoint(turn):
        with scope(f"g{turn}"):
            for start in range(0, cols, GROUP):
                group = col_peers[start:start + GROUP]
                for p in group:
                    if p is not col_peers[0]:
                        left_copy(turn, p, p).wait_recv()
                products = []
                for p in group:
                    for i in range(rays):
                        r = p * rays + i
                        row = left_panel[turn, p, i]
                        for k in range(per_block):
                            term = jnp.dot(row, tiles[r, k], preferred_element_type=f32)
                            products.append((1 + k * row_tiles + r, term))
                for t, term in products:
                    for h in range(HALVES):
                        terms[h, t] = term[:, h * half:(h + 1) * half]
        with scope(f"chain{turn}"):
            squares = jnp.zeros((sides, half), f32)
            for p in range(cols):
                squares = squares + left_panel[turn, p, rays, :, :half].astype(f32)
                squares = squares + left_panel[turn, p, rays, :, half:].astype(f32)
            high, low = split(squares)
            for h in range(HALVES):
                terms[h, 0] = jnp.zeros((sides, half), f32)

            def chain(r, k):
                before = table_ref[key_rows + k, r]
                for h in range(HALVES):
                    terms[h, 1 + k * row_tiles + r] = terms[h, 1 + k * row_tiles + r] + terms[h, before]

            for k in range(per_block):
                tile_loop(row_tiles, row_tiles, lambda r: chain(r, k))
        with scope(f"sendsums{turn}"):
            for n, (h, g) in enumerate(chunks):
                for p in reversed(row_peers[1:]):
                    def fill(i, n=n, h=h, g=g, p=p, share=share_of(p)):
                        term = terms[h, last_term(share, g * step_tiles + i)]
                        voxel_send[turn, n, p, i] = term.astype(bf16)

                    tile_loop(step_tiles, step_tiles, fill)
                    if n == 0:
                        voxel_send[turn, n, p, step_tiles] = high
                        voxel_send[turn, n, p, step_tiles + 1] = low
                    sums_copy(turn, n, p, p, me_row).start()
        voxel_recv[turn, 0, me_row, step_tiles] = high
        voxel_recv[turn, 0, me_row, step_tiles + 1] = low

    def sums_size(n):
        return pl.ds(0, step_tiles + 2 if n == 0 else step_tiles)

    def sums_copy(turn, n, peer, source, slot):
        return copy_to(
            "row", peer, voxel_send.at[turn, n, source, sums_size(n)], voxel_recv.at[turn, n, slot, sums_size(n)],
            vs_send_sem.at[n], vs_recv_sem.at[n],
        )

    def voxel_piece(n):
        h, g = chunks[n]
        return h, pl.ds(g * step_tiles, step_tiles + 2 if n == len(chunks) - 1 else step_tiles)

    def voxel_copy(turn, n, peer, slot):
        h, piece = voxel_piece(n)
        ref = voxel_panel[turn][h].at[slot, piece]
        return copy_to("row", peer, ref, ref, vp_send_sem.at[n], vp_recv_sem.at[n])

    def all_left(turn):
        whole = left_panel.at[turn, pl.ds(0, cols - 1)]
        return copy_to("col", col_peers[1], whole, whole, lp_send_sem, lp_recv_sem.at[0])

    def all_sums(turn, n):
        others = pl.ds(0, rows - 1)
        return copy_to(
            "row", row_peers[1], voxel_send.at[turn, n, others, sums_size(n)],
            voxel_recv.at[turn, n, others, sums_size(n)], vs_send_sem.at[n], vs_recv_sem.at[n],
        )

    def all_voxels(turn, n):
        h, piece = voxel_piece(n)
        whole = voxel_panel[turn][h].at[pl.ds(0, rows - 1), piece]
        return copy_to("row", row_peers[1], whole, whole, vp_send_sem.at[n], vp_recv_sem.at[n])

    def all_rays(turn):
        return copy_to(
            "col", col_peers[1], ray_send[turn].at[pl.ds(0, cols - 1)], ray_recv[turn].at[pl.ds(0, cols - 1)],
            rs_send_sem, rs_recv_sem,
        )

    def all_low(group):
        size = pl.ds(0, len(low_groups[group]))
        return copy_to(
            "row", row_peers[1], low_send.at[size], low_recv.at[size], lo_send_sem.at[group], lo_recv_sem.at[group]
        )

    def low_copy(group, peer, source, slot):
        return copy_to(
            "row", peer, low_send.at[source], low_recv.at[slot], lo_send_sem.at[group], lo_recv_sem.at[group]
        )

    def fill_low():
        for p in row_peers[1:]:
            share = share_of(p)
            for h in range(HALVES):
                for i in range(own):
                    term = terms[h, last_term(share, i)]
                    sent = voxel_send[0, h * STEPS + i // step_tiles, p, i % step_tiles]
                    low_send[p, h, i] = (term - sent.astype(f32)).astype(bf16)

    low_groups = (row_peers[1:max(rows // 2, 1)], row_peers[max(rows // 2, 1):])

    def send_low(group):
        for p in low_groups[group]:
            low_copy(group, p, p, me_row).start()

    def low_sum(group, h, i):
        total = low_recv[low_groups[group][0], h, i].astype(f32)
        for p in low_groups[group][1:]:
            total = total + low_recv[p, h, i].astype(f32)
        return total

    def add_low(group, inverse, pull=None):
        if not low_groups[group]:
            return
        all_low(group).wait_recv()

        def one(i):
            for h in range(HALVES):
                lanes = pl.ds(pl.multiple_of(i * tile_size + h * half, half), half)
                change = low_sum(group, h, i) * inverse
                first_ref[:, lanes] = first_ref[:, lanes] + change
                if pull is not None:
                    second_ref[:, lanes] = second_ref[:, lanes] - pull * change

        tile_loop(own, 4, one)

    right_refs = (first_ref, second_ref)

    def finish_right(turn, beta_of, alpha_before):
        beta = None
        my_share = share_of(me_row)
        squares = jnp.zeros((sides, half), f32)
        for n, (h, g) in enumerate(chunks):
            with scope(f"waitsums{turn}{n}"):
                all_sums(turn, n).wait_recv()
            if n == 0:
                beta, inverse, pull = beta_of()
            with scope(f"right{turn}{n}"):
                def one(i, squares, n=n, h=h, g=g):
                    at = g * step_tiles + i
                    total = terms[h, last_term(my_share, at)]
                    for p in row_peers[1:]:
                        total = total + voxel_recv[turn, n, p, i].astype(f32)
                    lanes = pl.ds(pl.multiple_of(at * tile_size + h * half, half), half)
                    right_raw = total * inverse
                    if turn > 0:
                        right_raw = right_raw - pull * right_refs[turn - 1][:, lanes]
                    right_refs[turn][:, lanes] = right_raw
                    voxel_panel[turn][h][me_row, at] = right_raw.astype(bf16)
                    return squares + right_raw * right_raw

                def step(base, squares):
                    for j in range(min(4, step_tiles)):
                        squares = one(base * min(4, step_tiles) + j, squares)
                    return squares

                squares = lax.fori_loop(0, step_tiles // min(4, step_tiles), step, squares)
                if n == len(chunks) - 1:
                    high, low = split(squares)
                    voxel_panel[turn][h][me_row, own] = high
                    voxel_panel[turn][h][me_row, own + 1] = low
                for p in reversed(row_peers[1:]):
                    voxel_copy(turn, n, p, me_row).start()
        return beta

    def beta_over_row(turn):
        total = jnp.zeros((sides, half), f32)
        for p in range(rows):
            total = total + voxel_recv[turn, 0, p, step_tiles].astype(f32)
            total = total + voxel_recv[turn, 0, p, step_tiles + 1].astype(f32)
        return norm_of(total)

    def ray_copy(turn, peer, source, slot):
        return copy_to(
            "col", peer, ray_send[turn].at[source], ray_recv[turn].at[slot],
            rs_send_sem, rs_recv_sem,
        )

    def picked(turn, h, r):
        pieces = []
        for k in range(per_block):
            c = cols_ref[k, r]
            pieces.append(voxel_panel[turn][h][place_of(c)])
        return jnp.concatenate(pieces, axis=1)

    def forward(turn):
        with scope(f"waitvox{turn}0"):
            for n in range(STEPS):
                all_voxels(turn, n).wait_recv()
        with scope(f"f{turn}0"):
            def early(r):
                ray_part[r] = jnp.dot(picked(turn, 0, r), turned[r, 0], preferred_element_type=f32)

            tile_loop(row_tiles, min(8, row_tiles), early)
        with scope(f"waitvox{turn}1"):
            for n in range(STEPS, len(chunks)):
                all_voxels(turn, n).wait_recv()
        with scope(f"f{turn}1"):
            squares = jnp.zeros((sides, half), f32)
            for p in range(rows):
                squares = squares + voxel_panel[turn][HALVES - 1][p, own].astype(f32)
                squares = squares + voxel_panel[turn][HALVES - 1][p, own + 1].astype(f32)
            kind = COL_SUMS[turn]

            def put_squares(ref, p):
                if kind == f32:
                    ref[p, HALVES * rays] = squares
                else:
                    high, low = split(squares)
                    ref[p, HALVES * rays] = high
                    ref[p, HALVES * rays + 1] = low

            def get_squares(p):
                if kind == f32:
                    return ray_recv[turn][p, HALVES * rays]
                return ray_recv[turn][p, HALVES * rays].astype(f32) + ray_recv[turn][p, HALVES * rays + 1].astype(f32)

            farthest = col_peers[::-1]
            for start in range(0, cols, GROUP):
                group = farthest[start:start + GROUP]
                products = []
                for p in group:
                    for i in range(rays):
                        r = p * rays + i
                        total = ray_part[r] + jnp.dot(picked(turn, 1, r), turned[r, 1], preferred_element_type=f32)
                        products.append((p, i, total))
                for p, i, total in products:
                    for h in range(HALVES):
                        ray_send[turn][p, HALVES * i + h] = total[:, h * half:(h + 1) * half].astype(kind)
                for p in group:
                    if p is not col_peers[0]:
                        put_squares(ray_send[turn], p)
                        ray_copy(turn, p, p, me_col).start()
            if turn == 0:
                send_low(0)
            put_squares(ray_recv[turn], me_col)
        with scope(f"waitrays{turn}"):
            pieces = [ray_send[turn][me_col, i].astype(f32) for i in range(HALVES * rays)]
            all_rays(turn).wait_recv()
            for p in col_peers[1:]:
                for i in range(HALVES * rays):
                    pieces[i] = pieces[i] + ray_recv[turn][p, i].astype(f32)
            squares = get_squares(0)
            for p in range(1, cols):
                squares = squares + get_squares(p)
        sums = [jnp.concatenate(pieces[HALVES * i:HALVES * (i + 1)], axis=1) for i in range(rays)]
        return sums, norm_of(squares)

    def wide(value):
        return jnp.concatenate([value] * HALVES, axis=1)

    def drain(turn):
        all_left(turn).wait_send()
        for n in range(len(chunks)):
            all_sums(turn, n).wait_send()
            all_voxels(turn, n).wait_send()
        all_rays(turn).wait_send()

    publish_left(0, [side_tile(i) for i in range(rays)])
    with scope("barrier"):
        pl.semaphore_wait(barrier, rows - 1 + cols - 1)
    send_left(0)
    with scope("table"):
        columns_load.wait()
        make_table()
    for part in range(LOAD_PARTS):
        load_part(part).wait()
    adjoint(0)
    with scope("turn"):
        for part in range(LOAD_PARTS // 2):
            turn_part(part)

    def first_beta():
        beta = beta_over_row(0)
        return beta, 1.0 / beta, None

    beta0 = finish_right(0, first_beta, None)
    with scope("turn2"):
        for part in range(LOAD_PARTS // 2, LOAD_PARTS):
            turn_part(part)
        fill_low()
    sums, alpha0 = forward(0)
    alpha = wide(alpha0)
    beta = wide(beta0)
    left_raw = [sums[i] / alpha - alpha * (side_tile(i) / beta) for i in range(rays)]
    for i in range(rays):
        left_ref[i] = left_raw[i]
    publish_left(1, left_raw)
    drain(0)
    send_left(1)
    adjoint(1)
    with scope("addlow"):
        add_low(0, 1.0 / beta0)

    def second_beta():
        beta = beta_over_row(1)
        return beta, 1.0 / beta, beta / alpha0

    beta1 = finish_right(1, second_beta, alpha0)
    rho1 = jnp.sqrt(alpha0 * alpha0 + beta1 * beta1)
    cosine1 = alpha0 / rho1
    sine1 = beta1 / rho1
    phi1 = cosine1 * beta0
    phibar1 = sine1 * beta0
    sums, alpha1 = forward(1)
    theta1 = sine1 * alpha1
    rhobar1 = -cosine1 * alpha1
    alpha = wide(alpha1)
    beta = wide(beta1)
    left_raw = [sums[i] / alpha - alpha * (left_ref[i] / beta) for i in range(rays)]
    for i in range(rays):
        left_ref[i] = left_raw[i]

    parts = 2 if cols == 16 else 1
    inner = cols // parts
    my_part = lax.div(me_col, inner)
    my_place = lax.rem(me_col, inner)
    place_peers = [(me_row, p, lax.rem(p, inner)) for p in col_peers[1:inner]]
    part_peers = []
    for d in range(parts):
        part = lax.rem(my_part + d, parts)
        for p in row_peers if d else row_peers[1:]:
            part_peers.append((p, part * inner + my_place, part * rows + p))

    def norm_copy(ref, peer, slot, send_sem, recv_sem):
        return pltpu.make_async_remote_copy(
            src_ref=ref.at[slot], dst_ref=ref.at[slot], send_sem=send_sem, recv_sem=recv_sem,
            device_id={"row": peer[0], "col": peer[1]}, device_id_type=MESH,
        )

    def all_sum(ref, peers, me, value, send_sem, recv_sem):
        ref[me] = value
        for peer in reversed(peers):
            norm_copy(ref, peer, me, send_sem, recv_sem).start()
        norm_copy(ref, peers[0], pl.ds(0, len(peers)), send_sem, recv_sem).wait()
        total = ref[0]
        for p in range(1, len(peers) + 1):
            total = total + ref[p]
        return total

    squares = fold(sum_of_squares(left_raw))
    send_low(1)
    with scope("normcol"):
        squares = all_sum(norm_col, place_peers, my_place, squares, nc_send_sem, nc_recv_sem)
    with scope("normrow"):
        squares = all_sum(norm_row, part_peers, my_part * rows + me_row, squares, nr_send_sem, nr_recv_sem)
    with scope("addlow2"):
        add_low(1, 1.0 / beta0, beta1 / alpha0)
    beta2 = norm_of(squares)
    rho2 = jnp.sqrt(rhobar1 * rhobar1 + beta2 * beta2)
    cosine2 = rhobar1 / rho2
    sine2 = beta2 / rho2
    phi2 = cosine2 * phibar1
    phibar2 = sine2 * phibar1
    for i, value in enumerate((
        alpha0, alpha1, phi1 / rho1, theta1 / rho1, phi2 / rho2, phibar2 / beta0, beta2, rho2, cosine2, sine2
    )):
        stats_ref[i] = value
    with scope("drain"):
        drain(1)
        for group in range(2):
            if low_groups[group]:
                all_low(group).wait_send()


def local(observed, tile_values, tile_cols):
    sides = observed.shape[0]
    row_tiles = tile_values.shape[0]
    per_block = tile_values.shape[1]
    tile_size = tile_values.shape[2]
    rows = lax.axis_size("row")
    cols = lax.axis_size("col")
    col_tiles = N // (tile_size * cols)
    panel_len = col_tiles * tile_size
    own = col_tiles // rows
    rays = row_tiles // cols
    flat = row_tiles * per_block
    half = tile_size // HALVES
    key_lanes = min(col_tiles, 128)
    key_rows = col_tiles // key_lanes

    f32 = jnp.float32
    bf16 = tile_values.dtype
    share_len = own * tile_size
    dma = pltpu.SemaphoreType.DMA
    voxel_shape = (ITERS, HALVES, rows, own + 2, sides, half)
    sums_shape = (ITERS, HALVES * STEPS, rows, own // STEPS + 2, sides, half)

    def ray_shape(kind):
        return (cols, HALVES * rays + (1 if kind == f32 else 2), sides, half)

    scratch = [
        pltpu.SMEM(tile_cols.shape[::-1], jnp.int32),
        pltpu.VMEM(tile_values.shape, bf16),
        pltpu.VMEM((row_tiles, HALVES, per_block * half, tile_size), bf16),
        pltpu.VMEM((HALVES, 1 + flat, sides, half), f32),
        pltpu.VMEM((row_tiles, sides, tile_size), f32),
        pltpu.VMEM((ITERS, cols, rays + 1, sides, tile_size), bf16),
        [[pltpu.VMEM(voxel_shape[2:], bf16) for _ in range(HALVES)] for _ in range(ITERS)],
        pltpu.VMEM(sums_shape, bf16),
        pltpu.VMEM(sums_shape, bf16),
        pltpu.VMEM((rows, HALVES, own, sides, half), bf16),
        pltpu.VMEM((rows, HALVES, own, sides, half), bf16),
        [pltpu.VMEM(ray_shape(kind), kind) for kind in COL_SUMS],
        [pltpu.VMEM(ray_shape(kind), kind) for kind in COL_SUMS],
        pltpu.VMEM((cols, sides, half), f32),
        pltpu.VMEM((2 * rows, sides, half), f32),
        pltpu.VMEM((key_rows + per_block, key_lanes), jnp.int32),
        pltpu.SMEM((key_rows + per_block, key_lanes), jnp.int32),
        dma, dma((LOAD_PARTS,)), dma,
        dma, dma((cols,)),
        dma((HALVES * STEPS,)), dma((HALVES * STEPS,)),
        dma((HALVES * STEPS,)), dma((HALVES * STEPS,)),
        dma((2,)), dma((2,)),
        dma, dma,
        dma, dma,
        dma, dma,
    ]
    vmem = pl.BlockSpec(memory_space=pltpu.VMEM)
    columns = jnp.transpose(tile_cols)
    first_raw, second_raw, left_raw, stats = pl.pallas_call(
        functools.partial(solver_kernel, rows, cols, rays, own),
        out_shape=(
            jax.ShapeDtypeStruct((sides, share_len), f32),
            jax.ShapeDtypeStruct((sides, share_len), f32),
            jax.ShapeDtypeStruct((rays, sides, tile_size), f32),
            jax.ShapeDtypeStruct((10, sides, half), f32),
        ),
        in_specs=[vmem, vmem, pl.BlockSpec(memory_space=pltpu.HBM)],
        out_specs=(vmem, vmem, vmem, vmem),
        scratch_shapes=scratch,
        compiler_params=pltpu.CompilerParams(
            collective_id=0, has_side_effects=True, vmem_limit_bytes=53 * 1024 * 1024
        ),
    )(observed, columns, tile_values)

    alpha0, alpha1, step1, turn1, step2, residual_ratio, beta2, rho2, cosine2, sine2 = (
        stats[i, :, :1] for i in range(10)
    )
    direction = first_raw / alpha0
    solution = step1 * direction
    right_vec = second_raw / alpha1
    direction = right_vec - turn1 * direction
    solution = solution + step2 * direction

    left_bf = jnp.transpose(left_raw, (1, 0, 2)).reshape(sides, -1).astype(bf16)
    gathered = lax.all_gather(left_bf, "col", axis=1, tiled=True).reshape(sides, row_tiles, tile_size)
    tile_terms = jnp.einsum("rktj,nrt->nrkj", tile_values, gathered, preferred_element_type=f32)
    placed = (
        jnp.zeros((sides, col_tiles, tile_size), f32)
        .at[:, tile_cols.reshape(-1)]
        .add(tile_terms.reshape(sides, flat, tile_size))
        .reshape(sides, panel_len)
    )
    product = lax.psum_scatter(placed, "row", scatter_dimension=1, tiled=True)
    last_raw = product / beta2 - beta2 * right_vec
    alpha2 = jnp.sqrt(lax.psum(jnp.sum(last_raw * last_raw, axis=1), ("row", "col")) + epsilon_sq)[:, None]
    theta2 = sine2 * alpha2
    rhobar2 = -cosine2 * alpha2
    direction = last_raw / alpha2 - (theta2 / rho2) * direction
    del direction, rhobar2
    return (solution, residual_ratio[:, 0])


def solution(mesh):
    in_specs = (P(None, ("row", "col")), P("row", "col", None, None), P("row", "col"))
    out_specs = (P(None, ("col", "row")), P())
    return jax.shard_map(local, mesh=mesh, in_specs=in_specs, out_specs=out_specs, check_vma=False)
```

```python
import functools

import jax
import jax.numpy as jnp
from jax import lax
from jax.experimental import pallas as pl
from jax.experimental.pallas import tpu as pltpu
from jax.sharding import PartitionSpec as P

ITERS = 2
N = 1048576

epsilon_sq = 1e-06

MESH = pl.DeviceIdType.MESH
COL_SUMS = (jnp.float32, jnp.bfloat16)
LOAD_PARTS = 8
GROUP = 8
HALVES = 2
CHAIN = 4
STEPS = 2


def scope(name):
    return jax.named_scope(name)


def norm_of(squares):
    total = jnp.sum(squares, axis=1, keepdims=True)
    return jnp.broadcast_to(jnp.sqrt(total + epsilon_sq), squares.shape)


def sum_of_squares(vectors):
    squares = vectors[0] * vectors[0]
    for vector in vectors[1:]:
        squares = squares + vector * vector
    return squares


def offsets(count):
    if count == 16:
        steps = [(z, x, c) for z in range(2) for x in range(4) for c in range(2)]
        return (8, 2, 1), (2, 4, 2), sorted(steps, key=lambda s: (2 * s[0] + min(s[1], 4 - s[1]), s))
    if count == 8:
        steps = [(z, y, 0) for z in range(2) for y in range(4)]
        return (4, 1, 1), (2, 4, 1), sorted(steps, key=lambda s: (s[0], min(s[1], 4 - s[1]), s))
    return (count, 1, 1), (1, count, 1), [(0, d, 0) for d in range(count)]


def peer_list(me, count):
    strides, sizes, steps = offsets(count)
    places = [lax.rem(lax.div(me, stride), size) for stride, size in zip(strides, sizes)]
    peers = []
    for step in steps:
        peer = 0
        for place, size, stride, d in zip(places, sizes, strides, step):
            if size > 1:
                peer = peer + lax.rem(place + d, size) * stride
        peers.append(peer)
    return peers


def solver_kernel(
    rows, cols, rays, own,
    observed_ref, cols_vec, tiles_hbm,
    first_ref, second_ref, left_ref, stats_ref,
    cols_ref, tiles, turned, terms, ray_part, left_panel, voxel_panel, voxel_send, voxel_recv, low_send, low_recv,
    ray_send, ray_recv, norm_col, norm_row, table_vec, table_ref,
    columns_sem, load_sem, table_sem, lp_send_sem, lp_recv_sem, vs_send_sem, vs_recv_sem, vp_send_sem, vp_recv_sem,
    lo_send_sem, lo_recv_sem, rs_send_sem, rs_recv_sem, nc_send_sem, nc_recv_sem, nr_send_sem, nr_recv_sem,
):
    f32 = jnp.float32
    bf16 = jnp.bfloat16
    me_row = lax.axis_index("row")
    me_col = lax.axis_index("col")
    row_tiles = tiles.shape[0]
    per_block = tiles.shape[1]
    tile_size = tiles.shape[2]
    half = tile_size // HALVES
    sides = observed_ref.shape[0]
    load_rows = row_tiles // LOAD_PARTS
    step_tiles = own // STEPS
    chunks = [(h, g) for h in range(HALVES) for g in range(STEPS)]
    flat = row_tiles * per_block
    key_rows = table_vec.shape[0] - per_block
    key_lanes = table_vec.shape[1]
    row_peers = peer_list(me_row, rows)
    col_peers = peer_list(me_col, cols)

    def copy_to(axis, peer, src, dst, send_sem, recv_sem):
        return pltpu.make_async_remote_copy(
            src_ref=src, dst_ref=dst, send_sem=send_sem, recv_sem=recv_sem,
            device_id={axis: peer}, device_id_type=MESH,
        )

    def each(me, count, body):
        def step(d, carry):
            body(lax.rem(me + d, count))
            return carry

        lax.fori_loop(1, count, step, 0)

    def tile_loop(count, unroll, body):
        def step(base, carry):
            for j in range(unroll):
                body(base * unroll + j)
            return carry

        lax.fori_loop(0, count // unroll, step, 0)

    def fold(squares):
        return squares[:, :half] + squares[:, half:]

    def split(value):
        high = value.astype(bf16)
        return high, (value - high.astype(f32)).astype(bf16)

    barrier = pltpu.get_barrier_semaphore()
    each(me_col, cols, lambda p: pl.semaphore_signal(barrier, inc=1, device_id={"col": p}, device_id_type=MESH))
    each(me_row, rows, lambda p: pl.semaphore_signal(barrier, inc=1, device_id={"row": p}, device_id_type=MESH))

    def load_part(part):
        piece = pl.ds(part * load_rows, load_rows)
        return pltpu.make_async_copy(tiles_hbm.at[piece], tiles.at[piece], load_sem.at[part])

    columns_load = pltpu.make_async_copy(cols_vec, cols_ref, columns_sem)
    columns_load.start()
    for part in range(LOAD_PARTS):
        load_part(part).start()

    def side_tile(i):
        return observed_ref[:, i * tile_size:(i + 1) * tile_size]

    def publish_left(turn, vectors):
        for i, vector in enumerate(vectors):
            left_panel[turn, me_col, i] = vector.astype(bf16)
        high, low = split(fold(sum_of_squares(vectors)))
        left_panel[turn, me_col, rays, :, :half] = high
        left_panel[turn, me_col, rays, :, half:] = low

    def left_copy(turn, peer, slot):
        return copy_to(
            "col", peer, left_panel.at[turn, slot], left_panel.at[turn, slot],
            lp_send_sem, lp_recv_sem.at[slot],
        )

    def send_left(turn):
        for p in reversed(col_peers[1:]):
            left_copy(turn, p, me_col).start()

    def make_table():
        columns = cols_vec[...]
        numbers = lax.broadcasted_iota(jnp.int32, columns.shape, 0) * row_tiles + lax.broadcasted_iota(
            jnp.int32, columns.shape, 1
        )
        key_shape = (key_rows, key_lanes)
        keys = lax.broadcasted_iota(jnp.int32, key_shape, 0) * key_lanes + lax.broadcasted_iota(jnp.int32, key_shape, 1)
        before = jnp.zeros_like(columns)
        last = jnp.zeros_like(keys)
        for t in range(flat):
            column = cols_ref[t // row_tiles, t % row_tiles]
            before = jnp.where((columns == column) & (numbers > t), t + 1, before)
            last = jnp.where(keys == column, t + 1, last)
        table_vec[...] = jnp.zeros_like(table_vec)
        table_vec[:key_rows, :] = last
        table_vec[key_rows:, :row_tiles] = before
        copy = pltpu.make_async_copy(table_vec, table_ref, table_sem)
        copy.start()
        copy.wait()

    def share_of(p):
        return lax.div(p * own, key_lanes), lax.rem(p * own, key_lanes)

    def last_term(share, i):
        return table_ref[share[0], share[1] + i]

    def place_of(c):
        if own & (own - 1):
            return lax.div(c, own), lax.rem(c, own)
        return lax.shift_right_logical(c, own.bit_length() - 1), c & (own - 1)

    def turn_part(part):
        for j in range(load_rows):
            r = part * load_rows + j
            for h in range(HALVES):
                for k in range(per_block):
                    block = tiles[r, k, :, h * half:(h + 1) * half]
                    turned[r, h, k * half:(k + 1) * half, :] = jnp.transpose(block)

    def adjoint(turn):
        with scope(f"g{turn}"):
            for start in range(0, cols, GROUP):
                group = col_peers[start:start + GROUP]
                for p in group:
                    if p is not col_peers[0]:
                        left_copy(turn, p, p).wait_recv()
                products = []
                for p in group:
                    for i in range(rays):
                        r = p * rays + i
                        row = left_panel[turn, p, i]
                        for k in range(per_block):
                            term = jnp.dot(row, tiles[r, k], preferred_element_type=f32)
                            products.append((1 + k * row_tiles + r, term))
                for t, term in products:
                    for h in range(HALVES):
                        terms[h, t] = term[:, h * half:(h + 1) * half]
        with scope(f"chain{turn}"):
            squares = jnp.zeros((sides, half), f32)
            for p in range(cols):
                squares = squares + left_panel[turn, p, rays, :, :half].astype(f32)
                squares = squares + left_panel[turn, p, rays, :, half:].astype(f32)
            high, low = split(squares)
            for h in range(HALVES):
                terms[h, 0] = jnp.zeros((sides, half), f32)

            def chain(start, k):
                slots = [1 + k * row_tiles + start + j for j in range(CHAIN)]
                before = [table_ref[key_rows + k, start + j] for j in range(CHAIN)]
                outside = [jnp.where(b >= slots[0], 0, b) for b in before]
                for h in range(HALVES):
                    sums = [terms[h, slots[j]] + terms[h, outside[j]] for j in range(CHAIN)]
                    for j in range(1, CHAIN):
                        for i in range(j):
                            sums[j] = sums[j] + jnp.where(before[j] == slots[i], sums[i], jnp.zeros_like(sums[i]))
                    for j in range(CHAIN):
                        terms[h, slots[j]] = sums[j]

            for k in range(per_block):
                for start in range(0, row_tiles, CHAIN):
                    chain(start, k)
        with scope(f"sendsums{turn}"):
            for n, (h, g) in enumerate(chunks):
                for p in reversed(row_peers[1:]):
                    def fill(i, n=n, h=h, g=g, p=p, share=share_of(p)):
                        term = terms[h, last_term(share, g * step_tiles + i)]
                        voxel_send[turn, n, p, i] = term.astype(bf16)

                    tile_loop(step_tiles, step_tiles, fill)
                    if n == 0:
                        voxel_send[turn, n, p, step_tiles] = high
                        voxel_send[turn, n, p, step_tiles + 1] = low
                    sums_copy(turn, n, p, p, me_row).start()
        voxel_recv[turn, 0, me_row, step_tiles] = high
        voxel_recv[turn, 0, me_row, step_tiles + 1] = low

    def sums_size(n):
        return pl.ds(0, step_tiles + 2 if n == 0 else step_tiles)

    def sums_copy(turn, n, peer, source, slot):
        return copy_to(
            "row", peer, voxel_send.at[turn, n, source, sums_size(n)], voxel_recv.at[turn, n, slot, sums_size(n)],
            vs_send_sem.at[n], vs_recv_sem.at[n],
        )

    def voxel_piece(n):
        h, g = chunks[n]
        return h, pl.ds(g * step_tiles, step_tiles + 2 if n == len(chunks) - 1 else step_tiles)

    def voxel_copy(turn, n, peer, slot):
        h, piece = voxel_piece(n)
        ref = voxel_panel[turn][h].at[slot, piece]
        return copy_to("row", peer, ref, ref, vp_send_sem.at[n], vp_recv_sem.at[n])

    def all_left(turn):
        whole = left_panel.at[turn, pl.ds(0, cols - 1)]
        return copy_to("col", col_peers[1], whole, whole, lp_send_sem, lp_recv_sem.at[0])

    def all_sums(turn, n):
        others = pl.ds(0, rows - 1)
        return copy_to(
            "row", row_peers[1], voxel_send.at[turn, n, others, sums_size(n)],
            voxel_recv.at[turn, n, others, sums_size(n)], vs_send_sem.at[n], vs_recv_sem.at[n],
        )

    def all_voxels(turn, n):
        h, piece = voxel_piece(n)
        whole = voxel_panel[turn][h].at[pl.ds(0, rows - 1), piece]
        return copy_to("row", row_peers[1], whole, whole, vp_send_sem.at[n], vp_recv_sem.at[n])

    def all_rays(turn):
        return copy_to(
            "col", col_peers[1], ray_send[turn].at[pl.ds(0, cols - 1)], ray_recv[turn].at[pl.ds(0, cols - 1)],
            rs_send_sem, rs_recv_sem,
        )

    def all_low(group):
        size = pl.ds(0, len(low_groups[group]))
        return copy_to(
            "row", row_peers[1], low_send.at[size], low_recv.at[size], lo_send_sem.at[group], lo_recv_sem.at[group]
        )

    def low_copy(group, peer, source, slot):
        return copy_to(
            "row", peer, low_send.at[source], low_recv.at[slot], lo_send_sem.at[group], lo_recv_sem.at[group]
        )

    def fill_low():
        for p in row_peers[1:]:
            share = share_of(p)
            for h in range(HALVES):
                for i in range(own):
                    term = terms[h, last_term(share, i)]
                    sent = voxel_send[0, h * STEPS + i // step_tiles, p, i % step_tiles]
                    low_send[p, h, i] = (term - sent.astype(f32)).astype(bf16)

    low_groups = (row_peers[1:max(rows // 2, 1)], row_peers[max(rows // 2, 1):])

    def send_low(group):
        for p in low_groups[group]:
            low_copy(group, p, p, me_row).start()

    def low_sum(group, h, i):
        total = low_recv[low_groups[group][0], h, i].astype(f32)
        for p in low_groups[group][1:]:
            total = total + low_recv[p, h, i].astype(f32)
        return total

    def add_low(group, inverse, pull=None):
        if not low_groups[group]:
            return
        all_low(group).wait_recv()

        def one(i):
            for h in range(HALVES):
                lanes = pl.ds(pl.multiple_of(i * tile_size + h * half, half), half)
                change = low_sum(group, h, i) * inverse
                first_ref[:, lanes] = first_ref[:, lanes] + change
                if pull is not None:
                    second_ref[:, lanes] = second_ref[:, lanes] - pull * change

        tile_loop(own, 4, one)

    right_refs = (first_ref, second_ref)

    def finish_right(turn, beta_of, alpha_before):
        beta = None
        my_share = share_of(me_row)
        squares = jnp.zeros((sides, half), f32)
        for n, (h, g) in enumerate(chunks):
            with scope(f"waitsums{turn}{n}"):
                all_sums(turn, n).wait_recv()
            if n == 0:
                beta, inverse, pull = beta_of()
            with scope(f"right{turn}{n}"):
                def one(i, squares, n=n, h=h, g=g):
                    at = g * step_tiles + i
                    total = terms[h, last_term(my_share, at)]
                    for p in row_peers[1:]:
                        total = total + voxel_recv[turn, n, p, i].astype(f32)
                    lanes = pl.ds(pl.multiple_of(at * tile_size + h * half, half), half)
                    right_raw = total * inverse
                    if turn > 0:
                        right_raw = right_raw - pull * right_refs[turn - 1][:, lanes]
                    right_refs[turn][:, lanes] = right_raw
                    voxel_panel[turn][h][me_row, at] = right_raw.astype(bf16)
                    return squares + right_raw * right_raw

                def step(base, squares):
                    for j in range(min(4, step_tiles)):
                        squares = one(base * min(4, step_tiles) + j, squares)
                    return squares

                squares = lax.fori_loop(0, step_tiles // min(4, step_tiles), step, squares)
                if n == len(chunks) - 1:
                    high, low = split(squares)
                    voxel_panel[turn][h][me_row, own] = high
                    voxel_panel[turn][h][me_row, own + 1] = low
                for p in reversed(row_peers[1:]):
                    voxel_copy(turn, n, p, me_row).start()
        return beta

    def beta_over_row(turn):
        total = jnp.zeros((sides, half), f32)
        for p in range(rows):
            total = total + voxel_recv[turn, 0, p, step_tiles].astype(f32)
            total = total + voxel_recv[turn, 0, p, step_tiles + 1].astype(f32)
        return norm_of(total)

    def ray_copy(turn, peer, source, slot):
        return copy_to(
            "col", peer, ray_send[turn].at[source], ray_recv[turn].at[slot],
            rs_send_sem, rs_recv_sem,
        )

    def picked(turn, h, r):
        pieces = []
        for k in range(per_block):
            c = cols_ref[k, r]
            pieces.append(voxel_panel[turn][h][place_of(c)])
        return jnp.concatenate(pieces, axis=1)

    def forward(turn):
        with scope(f"waitvox{turn}0"):
            for n in range(STEPS):
                all_voxels(turn, n).wait_recv()
        with scope(f"f{turn}0"):
            def early(r):
                ray_part[r] = jnp.dot(picked(turn, 0, r), turned[r, 0], preferred_element_type=f32)

            tile_loop(row_tiles, min(8, row_tiles), early)
        with scope(f"waitvox{turn}1"):
            for n in range(STEPS, len(chunks)):
                all_voxels(turn, n).wait_recv()
        with scope(f"f{turn}1"):
            squares = jnp.zeros((sides, half), f32)
            for p in range(rows):
                squares = squares + voxel_panel[turn][HALVES - 1][p, own].astype(f32)
                squares = squares + voxel_panel[turn][HALVES - 1][p, own + 1].astype(f32)
            kind = COL_SUMS[turn]

            def put_squares(ref, p):
                if kind == f32:
                    ref[p, HALVES * rays] = squares
                else:
                    high, low = split(squares)
                    ref[p, HALVES * rays] = high
                    ref[p, HALVES * rays + 1] = low

            def get_squares(p):
                if kind == f32:
                    return ray_recv[turn][p, HALVES * rays]
                return ray_recv[turn][p, HALVES * rays].astype(f32) + ray_recv[turn][p, HALVES * rays + 1].astype(f32)

            farthest = col_peers[::-1]
            for start in range(0, cols, GROUP):
                group = farthest[start:start + GROUP]
                products = []
                for p in group:
                    for i in range(rays):
                        r = p * rays + i
                        total = ray_part[r] + jnp.dot(picked(turn, 1, r), turned[r, 1], preferred_element_type=f32)
                        products.append((p, i, total))
                for p, i, total in products:
                    for h in range(HALVES):
                        ray_send[turn][p, HALVES * i + h] = total[:, h * half:(h + 1) * half].astype(kind)
                for p in group:
                    if p is not col_peers[0]:
                        put_squares(ray_send[turn], p)
                        ray_copy(turn, p, p, me_col).start()
            if turn == 0:
                send_low(0)
            put_squares(ray_recv[turn], me_col)
        with scope(f"waitrays{turn}"):
            pieces = [ray_send[turn][me_col, i].astype(f32) for i in range(HALVES * rays)]
            all_rays(turn).wait_recv()
            for p in col_peers[1:]:
                for i in range(HALVES * rays):
                    pieces[i] = pieces[i] + ray_recv[turn][p, i].astype(f32)
            squares = get_squares(0)
            for p in range(1, cols):
                squares = squares + get_squares(p)
        sums = [jnp.concatenate(pieces[HALVES * i:HALVES * (i + 1)], axis=1) for i in range(rays)]
        return sums, norm_of(squares)

    def wide(value):
        return jnp.concatenate([value] * HALVES, axis=1)

    def drain(turn):
        all_left(turn).wait_send()
        for n in range(len(chunks)):
            all_sums(turn, n).wait_send()
            all_voxels(turn, n).wait_send()
        all_rays(turn).wait_send()

    publish_left(0, [side_tile(i) for i in range(rays)])
    with scope("barrier"):
        pl.semaphore_wait(barrier, rows - 1 + cols - 1)
    send_left(0)
    with scope("table"):
        columns_load.wait()
        make_table()
    for part in range(LOAD_PARTS):
        load_part(part).wait()
    adjoint(0)
    with scope("turn"):
        for part in range(LOAD_PARTS // 2):
            turn_part(part)

    def first_beta():
        beta = beta_over_row(0)
        return beta, 1.0 / beta, None

    beta0 = finish_right(0, first_beta, None)
    with scope("turn2"):
        for part in range(LOAD_PARTS // 2, LOAD_PARTS):
            turn_part(part)
        fill_low()
    sums, alpha0 = forward(0)
    alpha = wide(alpha0)
    beta = wide(beta0)
    left_raw = [sums[i] / alpha - alpha * (side_tile(i) / beta) for i in range(rays)]
    for i in range(rays):
        left_ref[i] = left_raw[i]
    publish_left(1, left_raw)
    drain(0)
    send_left(1)
    adjoint(1)
    with scope("addlow"):
        add_low(0, 1.0 / beta0)

    def second_beta():
        beta = beta_over_row(1)
        return beta, 1.0 / beta, beta / alpha0

    beta1 = finish_right(1, second_beta, alpha0)
    rho1 = jnp.sqrt(alpha0 * alpha0 + beta1 * beta1)
    cosine1 = alpha0 / rho1
    sine1 = beta1 / rho1
    phi1 = cosine1 * beta0
    phibar1 = sine1 * beta0
    sums, alpha1 = forward(1)
    theta1 = sine1 * alpha1
    rhobar1 = -cosine1 * alpha1
    alpha = wide(alpha1)
    beta = wide(beta1)
    left_raw = [sums[i] / alpha - alpha * (left_ref[i] / beta) for i in range(rays)]
    for i in range(rays):
        left_ref[i] = left_raw[i]

    parts = 2 if cols == 16 else 1
    inner = cols // parts
    my_part = lax.div(me_col, inner)
    my_place = lax.rem(me_col, inner)
    place_peers = [(me_row, p, lax.rem(p, inner)) for p in col_peers[1:inner]]
    part_peers = []
    for d in range(parts):
        part = lax.rem(my_part + d, parts)
        for p in row_peers if d else row_peers[1:]:
            part_peers.append((p, part * inner + my_place, part * rows + p))

    def norm_copy(ref, peer, slot, send_sem, recv_sem):
        return pltpu.make_async_remote_copy(
            src_ref=ref.at[slot], dst_ref=ref.at[slot], send_sem=send_sem, recv_sem=recv_sem,
            device_id={"row": peer[0], "col": peer[1]}, device_id_type=MESH,
        )

    def start_sum(ref, peers, me, value, send_sem, recv_sem):
        ref[me] = value
        for peer in reversed(peers):
            norm_copy(ref, peer, me, send_sem, recv_sem).start()

    def end_sum(ref, peers, send_sem, recv_sem):
        norm_copy(ref, peers[0], pl.ds(0, len(peers)), send_sem, recv_sem).wait()
        total = ref[0]
        for p in range(1, len(peers) + 1):
            total = total + ref[p]
        return total

    squares = fold(sum_of_squares(left_raw))
    with scope("normcol"):
        start_sum(norm_col, place_peers, my_place, squares, nc_send_sem, nc_recv_sem)
        send_low(1)
        squares = end_sum(norm_col, place_peers, nc_send_sem, nc_recv_sem)
    with scope("normrow"):
        start_sum(norm_row, part_peers, my_part * rows + me_row, squares, nr_send_sem, nr_recv_sem)
    with scope("addlow2"):
        add_low(1, 1.0 / beta0, beta1 / alpha0)
    with scope("normrow2"):
        squares = end_sum(norm_row, part_peers, nr_send_sem, nr_recv_sem)
    beta2 = norm_of(squares)
    rho2 = jnp.sqrt(rhobar1 * rhobar1 + beta2 * beta2)
    cosine2 = rhobar1 / rho2
    sine2 = beta2 / rho2
    phi2 = cosine2 * phibar1
    phibar2 = sine2 * phibar1
    for i, value in enumerate((
        alpha0, alpha1, phi1 / rho1, theta1 / rho1, phi2 / rho2, phibar2 / beta0, beta2, rho2, cosine2, sine2
    )):
        stats_ref[i] = value
    with scope("drain"):
        drain(1)
        for group in range(2):
            if low_groups[group]:
                all_low(group).wait_send()


def local(observed, tile_values, tile_cols):
    sides = observed.shape[0]
    row_tiles = tile_values.shape[0]
    per_block = tile_values.shape[1]
    tile_size = tile_values.shape[2]
    rows = lax.axis_size("row")
    cols = lax.axis_size("col")
    col_tiles = N // (tile_size * cols)
    panel_len = col_tiles * tile_size
    own = col_tiles // rows
    rays = row_tiles // cols
    flat = row_tiles * per_block
    half = tile_size // HALVES
    key_lanes = min(col_tiles, 128)
    key_rows = col_tiles // key_lanes

    f32 = jnp.float32
    bf16 = tile_values.dtype
    share_len = own * tile_size
    dma = pltpu.SemaphoreType.DMA
    voxel_shape = (ITERS, HALVES, rows, own + 2, sides, half)
    sums_shape = (ITERS, HALVES * STEPS, rows, own // STEPS + 2, sides, half)

    def ray_shape(kind):
        return (cols, HALVES * rays + (1 if kind == f32 else 2), sides, half)

    scratch = [
        pltpu.SMEM(tile_cols.shape[::-1], jnp.int32),
        pltpu.VMEM(tile_values.shape, bf16),
        pltpu.VMEM((row_tiles, HALVES, per_block * half, tile_size), bf16),
        pltpu.VMEM((HALVES, 1 + flat, sides, half), f32),
        pltpu.VMEM((row_tiles, sides, tile_size), f32),
        pltpu.VMEM((ITERS, cols, rays + 1, sides, tile_size), bf16),
        [[pltpu.VMEM(voxel_shape[2:], bf16) for _ in range(HALVES)] for _ in range(ITERS)],
        pltpu.VMEM(sums_shape, bf16),
        pltpu.VMEM(sums_shape, bf16),
        pltpu.VMEM((rows, HALVES, own, sides, half), bf16),
        pltpu.VMEM((rows, HALVES, own, sides, half), bf16),
        [pltpu.VMEM(ray_shape(kind), kind) for kind in COL_SUMS],
        [pltpu.VMEM(ray_shape(kind), kind) for kind in COL_SUMS],
        pltpu.VMEM((cols, sides, half), f32),
        pltpu.VMEM((2 * rows, sides, half), f32),
        pltpu.VMEM((key_rows + per_block, key_lanes), jnp.int32),
        pltpu.SMEM((key_rows + per_block, key_lanes), jnp.int32),
        dma, dma((LOAD_PARTS,)), dma,
        dma, dma((cols,)),
        dma((HALVES * STEPS,)), dma((HALVES * STEPS,)),
        dma((HALVES * STEPS,)), dma((HALVES * STEPS,)),
        dma((2,)), dma((2,)),
        dma, dma,
        dma, dma,
        dma, dma,
    ]
    vmem = pl.BlockSpec(memory_space=pltpu.VMEM)
    columns = jnp.transpose(tile_cols)
    first_raw, second_raw, left_raw, stats = pl.pallas_call(
        functools.partial(solver_kernel, rows, cols, rays, own),
        out_shape=(
            jax.ShapeDtypeStruct((sides, share_len), f32),
            jax.ShapeDtypeStruct((sides, share_len), f32),
            jax.ShapeDtypeStruct((rays, sides, tile_size), f32),
            jax.ShapeDtypeStruct((10, sides, half), f32),
        ),
        in_specs=[vmem, vmem, pl.BlockSpec(memory_space=pltpu.HBM)],
        out_specs=(vmem, vmem, vmem, vmem),
        scratch_shapes=scratch,
        compiler_params=pltpu.CompilerParams(
            collective_id=0, has_side_effects=True, vmem_limit_bytes=53 * 1024 * 1024
        ),
    )(observed, columns, tile_values)

    alpha0, alpha1, step1, turn1, step2, residual_ratio, beta2, rho2, cosine2, sine2 = (
        stats[i, :, :1] for i in range(10)
    )
    direction = first_raw / alpha0
    solution = step1 * direction
    right_vec = second_raw / alpha1
    direction = right_vec - turn1 * direction
    solution = solution + step2 * direction

    left_bf = jnp.transpose(left_raw, (1, 0, 2)).reshape(sides, -1).astype(bf16)
    gathered = lax.all_gather(left_bf, "col", axis=1, tiled=True).reshape(sides, row_tiles, tile_size)
    tile_terms = jnp.einsum("rktj,nrt->nrkj", tile_values, gathered, preferred_element_type=f32)
    placed = (
        jnp.zeros((sides, col_tiles, tile_size), f32)
        .at[:, tile_cols.reshape(-1)]
        .add(tile_terms.reshape(sides, flat, tile_size))
        .reshape(sides, panel_len)
    )
    product = lax.psum_scatter(placed, "row", scatter_dimension=1, tiled=True)
    last_raw = product / beta2 - beta2 * right_vec
    alpha2 = jnp.sqrt(lax.psum(jnp.sum(last_raw * last_raw, axis=1), ("row", "col")) + epsilon_sq)[:, None]
    theta2 = sine2 * alpha2
    rhobar2 = -cosine2 * alpha2
    direction = last_raw / alpha2 - (theta2 / rho2) * direction
    del direction, rhobar2
    return (solution, residual_ratio[:, 0])


def solution(mesh):
    in_specs = (P(None, ("row", "col")), P("row", "col", None, None), P("row", "col"))
    out_specs = (P(None, ("col", "row")), P())
    return jax.shard_map(local, mesh=mesh, in_specs=in_specs, out_specs=out_specs, check_vma=False)
```
